256 devices in a mesh: member: 8 (over x, z_hi), slab: 32 (over y, z_lo, core).
Axes of the slice: x: 4, y: 4, z: 8 (z_hi: 2, z_lo: 4; z = z_hi * 4 + z_lo), core: 2. Of those that a mesh axis runs over, the one named last changes fastest.
Arguments:
- prior_ensemble_fields: float32 [64, 6, 256, 1, 1024], P('member', None, 'slab'), may hold values from -6 to 6
- params: float32 [64, 12], P('member'), may hold values from -3 to 3
- influence: int32 [12, 6], replicated, may hold values 0 or 1
- obs_cell: int32 [256, 8, 128], P('slab', 'member'), may hold values from 0 to 767
- obs_value: float32 [256, 8, 128], P('slab', 'member'), may hold values from -6 to 6
- obs_prec: float32 [256, 8, 128], P('slab', 'member'), may hold values from 0.5 to 4
- cutoff: int32 [256], P('slab'), may hold values from 4 to 8, as said below
Outputs:
- analysis: bfloat16 [64, 6, 256, 1, 1024], P('member', None, 'slab')
- param_analysis: float32 [64, 12], P('member')
The draws below stay inside these ranges and needn't reach their ends.
Inputs may be any that keep to these rules, and one draw needn't show every extreme that they name: `obs_cell`: index = field * 128 + level * 128 + column within the block. `cutoff`: 8 is reached by some rows.
All inputs are finite; a program needn't handle non-finite values.
Results may differ from the reference program's by a relative error of at most 0.0056.
Values may be sent and summed in bfloat16 or wider, within the bound.
A program may use at most 64 MiB of HBM per device.

```python
import math
import jax
import jax.numpy as jnp
from jax import lax

ENS = 64
FIELDS = 6
NPAR = 12
LEV = 1
COLS = 1024
HALO = 8
NOBS = 128
STEPS = 4
NS_STEPS = 5
NY = 256
NBLK = 8
CB = 128


def draw_cutoff(key, part):
    first_key = jax.random.fold_in(key, 11)
    second_key = jax.random.fold_in(key, 23)
    values = jax.random.randint(first_key, (NY,), HALO // 2, HALO + 1)
    order = jax.random.permutation(second_key, NY)
    chosen = order[:max(1, NY // 8)]
    values = values.at[chosen].set(HALO)
    return values.astype(jnp.int32)


def set_ends(entries, rng, smallest, largest):
    extent = entries.shape
    index_at = [jax.random.randint(jax.random.fold_in(rng, axis), (), 0, extent[axis]) for axis in range(len(extent))]
    entries = entries.at[tuple(index_at)].set(smallest)
    longest = extent.index(max(extent))
    index_at[longest] = (index_at[longest] + 1) % extent[longest]
    return entries.at[tuple(index_at)].set(largest)


def steps_of(stream_key, extent, split, smallest, largest):
    gain = 1.0
    for position, shards_of in split:
        heights = jax.random.uniform(jax.random.fold_in(jax.random.fold_in(stream_key, 6), position), (shards_of,), jnp.float32, smallest / len(split), largest / len(split))
        gain = gain * jnp.repeat(jnp.exp(heights), extent[position] // shards_of).reshape((-1,) + (1,) * (len(extent) - 1 - position))
    return gain


def noise(rng, dims, deviation, reach, shards=(), kind=jnp.bfloat16):
    array = deviation * jax.random.normal(rng, dims, jnp.float32)
    if shards:
        array = array * steps_of(rng, dims, shards, -0.22, 0.18)
    return jnp.clip(array, -reach, reach).astype(kind)


def setup_inputs(seed: int = 0) -> dict:
    keys = jax.random.split(jax.random.key(seed), 8)
    return {
        "prior_ensemble_fields": noise(keys[0], (ENS, FIELDS, NY, LEV, COLS), 1.0, 6.0, ((0, 8), (2, 32)), jnp.float32),
        "params": noise(keys[1], (ENS, NPAR), 0.5, 3.0, ((0, 8),), jnp.float32),
        "influence": set_ends((jax.random.randint(keys[2], (NPAR, FIELDS), 0, 2) < 1).astype(jnp.int32), jax.random.fold_in(keys[2], 1), 0, 1),
        "obs_cell": set_ends(jax.random.randint(keys[3], (NY, NBLK, NOBS), 0, FIELDS * LEV * CB), jax.random.fold_in(keys[3], 1), 0, (FIELDS * LEV * CB) - 1).astype(jnp.int32),
        "obs_value": noise(keys[4], (NY, NBLK, NOBS), 1.5, 6.0, ((0, 32), (1, 8)), jnp.float32),
        "obs_prec": jnp.clip(jnp.exp(math.log(4.0) - 2.0794415 * jax.random.uniform(keys[5], (NY, NBLK, NOBS), jnp.float32) ** steps_of(keys[5], (NY, NBLK, NOBS), ((0, 32), (1, 8)), -0.2, 0.2)), 0.5, 4.0),
        "cutoff": draw_cutoff(jax.random.fold_in(keys[7], 71), 0),
    }


diffusion = 0.2
advection = 0.15
vertical = 0.1
coupling = 0.2

def stencil_step(prognostic_vector, coef_row):
    zero_row = jnp.zeros_like(prognostic_vector[:, :1])
    upper = jnp.concatenate([prognostic_vector[:, 1:], zero_row], 1)
    lower = jnp.concatenate([zero_row, prognostic_vector[:, :-1]], 1)
    right_col = jnp.roll(prognostic_vector, -1, 3)
    left_col = jnp.roll(prognostic_vector, 1, 3)
    laplace = upper + lower + right_col + left_col - 4.0 * prognostic_vector
    return prognostic_vector + diffusion * laplace - advection * (right_col - left_col) + vertical * (jnp.roll(prognostic_vector, 1, 2) - prognostic_vector) + coupling * coef_row[:, None, None, None] * jnp.roll(prognostic_vector, -1, 0)

def propagate_single_trajectory(incoming_grids):
    prognostic_vector, coef_row = incoming_grids
    for step_idx in range(STEPS):
        prognostic_vector = stencil_step(prognostic_vector, coef_row)
    return prognostic_vector.astype(jnp.bfloat16)

def newton_roots(amat):
    highest = lax.Precision.HIGHEST
    ensemble = amat.shape[-1]
    eye_mat = jnp.eye(ensemble, dtype=jnp.float32)
    scale = jnp.sqrt(lax.optimization_barrier(jnp.sum(amat * amat, axis=(-2, -1))))
    ymat = amat / scale[..., None, None]
    zmat = jnp.broadcast_to(eye_mat, amat.shape)
    for step_idx in range(NS_STEPS):
        middle = 1.5 * eye_mat - 0.5 * jnp.matmul(zmat, ymat, precision=highest)
        ymat = jnp.matmul(ymat, middle, precision=highest)
        zmat = jnp.matmul(middle, zmat, precision=highest)
    return (zmat, scale)

def reference(prior_ensemble_fields, params, influence, obs_cell, obs_value, obs_prec, cutoff):
    highest = lax.Precision.HIGHEST
    dynamics_parameter = jnp.dot(params, influence.astype(jnp.float32), precision=highest)
    propagate_timestep = lax.map(propagate_single_trajectory, (prior_ensemble_fields, dynamics_parameter))

    def row_gram(latitude_offset):
        band_prognostic_entries = lax.dynamic_index_in_dim(propagate_timestep, latitude_offset, 2, keepdims=False).astype(jnp.float32)
        band_prognostic_entries = band_prognostic_entries.reshape(ENS, FIELDS, LEV, NBLK, CB)
        cells = lax.dynamic_index_in_dim(obs_cell, latitude_offset, 0, keepdims=False)
        values = lax.dynamic_index_in_dim(obs_value, latitude_offset, 0, keepdims=False)
        precs = lax.dynamic_index_in_dim(obs_prec, latitude_offset, 0, keepdims=False)
        kinds = cells // (LEV * CB)
        levels = cells // CB % LEV
        columns = cells % CB
        blocks = jnp.arange(NBLK, dtype=jnp.int32)[:, None]
        ens_obs = band_prognostic_entries[:, kinds, levels, blocks, columns]
        ybar = lax.optimization_barrier(jnp.mean(ens_obs, axis=0))
        ypert = ens_obs - ybar
        weighted = precs * (values - ybar)
        gram = jnp.einsum('ebo,fbo->bef', ypert * precs[None], ypert, precision=highest)
        gvec = jnp.einsum('ebo,bo->be', ypert, weighted, precision=highest)
        return jnp.concatenate([gram, gvec[:, None, :]], 1)
    stacked = lax.map(row_gram, jnp.arange(NY, dtype=jnp.int32))
    padded = jnp.pad(stacked, ((HALO, HALO), (0, 0), (0, 0), (0, 0)))
    radius = cutoff.astype(jnp.float32)
    local = jnp.zeros_like(stacked)
    for offset in range(-HALO, HALO + 1):
        weight = jnp.maximum(0.0, 1.0 - abs(offset) / (radius + 1.0))
        local = local + weight[:, None, None, None] * padded[HALO + offset:HALO + offset + NY]
    gram_loc = local[:, :, :ENS]
    gvec_loc = local[:, :, ENS]
    amat = (ENS - 1.0) * jnp.eye(ENS, dtype=jnp.float32) + gram_loc
    zmat, scale = newton_roots(amat)
    wpert = math.sqrt(ENS - 1.0) * zmat / jnp.sqrt(scale)[..., None, None]
    inner = jnp.matmul(zmat, gvec_loc[..., None], precision=highest)
    wbar = jnp.matmul(zmat, inner, precision=highest)[..., 0] / scale[..., None]
    weights = wpert + wbar[..., None]

    def row_update(incoming_grids):
        latitude_offset, row_weights = incoming_grids
        band_prognostic_entries = lax.dynamic_index_in_dim(propagate_timestep, latitude_offset, 2, keepdims=False).astype(jnp.float32)
        band_prognostic_entries = band_prognostic_entries.reshape(ENS, FIELDS, LEV, NBLK, CB)
        xbar = lax.optimization_barrier(jnp.mean(band_prognostic_entries, axis=0))
        xpert = band_prognostic_entries - xbar
        update = jnp.einsum('jflbc,bje->eflbc', xpert, row_weights, precision=highest)
        return (xbar + update).astype(jnp.bfloat16).reshape(ENS, FIELDS, LEV, COLS)
    rows_out = lax.map(row_update, (jnp.arange(NY, dtype=jnp.int32), weights))
    analysis = jnp.moveaxis(rows_out, 0, 2)
    wmean = lax.optimization_barrier(jnp.sum(weights, axis=(0, 1))) / (NY * NBLK)
    pbar = lax.optimization_barrier(jnp.mean(params, axis=0))
    ppert = params - pbar
    param_analysis = pbar + jnp.einsum('jk,je->ek', ppert, wmean, precision=highest)
    return (analysis, param_analysis)
```

```python
import math

import jax
import jax.numpy as jnp
from jax import lax
from jax.experimental import pallas as pl
from jax.experimental.pallas import tpu as pltpu
from jax.sharding import PartitionSpec as P

STEPS = 4
HALO = 8
NS_STEPS = 5
MESH = pl.DeviceIdType.MESH
F32 = jnp.float32
BF16 = jnp.bfloat16

diffusion = 0.2
advection = 0.15
vertical = 0.1
coupling = 0.2

M = 8
F = 6
R = 8
T = 8
LANES = 128
ENS = 64
W = STEPS


def split(a):
    high = a.astype(BF16)
    return high, (a - high.astype(F32)).astype(BF16)


def dot(a, b):
    return jnp.dot(a, b, preferred_element_type=F32)


def dot_nt(a, b):
    return lax.dot_general(a, b, (((1,), (1,)), ((), ())), preferred_element_type=F32)


def mm(left, right):
    lh, ll = split(left)
    rh, rl = split(right)
    return dot(lh, rh) + (dot(lh, rl) + dot(ll, rh))


def mm_nt(left, right):
    lh, ll = split(left)
    rh, rl = split(right)
    return dot_nt(lh, rh) + (dot_nt(lh, rl) + dot_nt(ll, rh))


def kernel(
    slabs,
    group,
    x_ref, params_ref, infl_ref, cell_ref, value_ref, prec_ref, cut_ref,
    out_ref, pout_ref,
    s0, s1, s2, s3, hs, hr, xs, xr, ys, yr, oc, pv, pp, gs, am, os_, ps, ra, rb, rc,
    load_sem, halo_send, halo_recv, pv_send, pv_recv, oc_send, oc_recv, pp_send, pp_recv,
    ys_send, ys_recv, yf_send, yf_recv, xs_send, xs_recv, os_send, os_recv,
    ra_send, ra_recv, rb_send, rb_recv, rc_send, rc_recv, own_sem,
):
    mu = lax.axis_index("member")
    sl = lax.axis_index("slab")
    has_low = sl > 0
    has_high = sl < slabs - 1
    bands = slabs // group
    band, place = sl // group, lax.rem(sl, group)

    loads = []
    for f in range(F):
        for m in range(M):
            copy = pltpu.make_async_copy(
                x_ref.at[m, f], s0.at[f, pl.ds(W, R), :, m, :], load_sem.at[f, m]
            )
            copy.start()
            loads.append(copy)

    barrier = pltpu.get_barrier_semaphore()
    others = [lax.rem(mu + i, M) for i in range(M)]
    for i in range(1, M):
        pl.semaphore_signal(barrier, inc=1, device_id=(others[i], sl), device_id_type=MESH)
    for i in range(1, group):
        peer = band * group + lax.rem(place + i, group)
        pl.semaphore_signal(barrier, inc=1, device_id=(mu, peer), device_id_type=MESH)
    for i in range(1, bands):
        peer = lax.rem(sl + i * group, slabs)
        pl.semaphore_signal(barrier, inc=1, device_id=(mu, peer), device_id_type=MESH)

    @pl.when(has_low)
    def _():
        pl.semaphore_signal(barrier, inc=1, device_id=(mu, sl - 1), device_id_type=MESH)

    @pl.when(has_high)
    def _():
        pl.semaphore_signal(barrier, inc=1, device_id=(mu, sl + 1), device_id_type=MESH)

    expected = (M - 1) + (group - 1) + (bands - 1)
    expected = expected + jnp.where(has_low, 1, 0) + jnp.where(has_high, 1, 0)
    pl.semaphore_wait(barrier, expected)

    def halo_copy(side, f):
        peer = sl - 1 if side == 0 else sl + 1
        return pltpu.make_async_remote_copy(
            src_ref=hs.at[side, f], dst_ref=hr.at[1 - side, f],
            send_sem=halo_send.at[side, f], recv_sem=halo_recv.at[1 - side, f],
            device_id=(mu, peer), device_id_type=MESH,
        )

    for f in range(F):
        for m in range(M):
            loads[f * M + m].wait()
        for side in range(2):
            for q in range(2):
                row = W + 4 * side + 2 * q
                pair = jnp.concatenate([s0[f, row], s0[f, row + 1]], axis=1)
                hs[side, f, q] = pair.astype(BF16)

        @pl.when(has_low)
        def _():
            halo_copy(0, f).start()

        @pl.when(has_high)
        def _():
            halo_copy(1, f).start()

    pp[mu] = jnp.zeros((M, LANES), F32)
    pp[mu, :, : params_ref.shape[1]] = params_ref[...]
    oc[mu] = cell_ref[...]
    pv[0, 0] = prec_ref[...]
    pv[0, 1] = value_ref[...]

    def pp_copy(i):
        return pltpu.make_async_remote_copy(
            src_ref=pp.at[mu], dst_ref=pp.at[mu], send_sem=pp_send.at[i], recv_sem=pp_recv.at[i],
            device_id=(others[i], sl), device_id_type=MESH,
        )

    def oc_copy(i):
        return pltpu.make_async_remote_copy(
            src_ref=oc.at[mu], dst_ref=oc.at[mu], send_sem=oc_send.at[i], recv_sem=oc_recv.at[i],
            device_id=(others[i], sl), device_id_type=MESH,
        )

    def pv_copy(side):
        peer = sl - 1 if side == 0 else sl + 1
        return pltpu.make_async_remote_copy(
            src_ref=pv.at[0], dst_ref=pv.at[2 - side], send_sem=pv_send.at[side], recv_sem=pv_recv.at[1 - side],
            device_id=(mu, peer), device_id_type=MESH,
        )

    for i in range(1, M):
        oc_copy(i).start()
        pp_copy(i).start()

    @pl.when(has_low)
    def _():
        pv_copy(0).start()

    @pl.when(has_high)
    def _():
        pv_copy(1).start()

    coef = lax.dot_general(
        params_ref[...], infl_ref[...].astype(F32), (((1,), (1,)), ((), ())),
        precision=lax.Precision.HIGHEST, preferred_element_type=F32,
    )
    pull = [jnp.broadcast_to(coupling * coef[:, f : f + 1], (M, LANES))[None] for f in range(F)]
    lane = lax.broadcasted_iota(jnp.int32, (T, M, LANES), 2)
    first, last = lane == 0, lane == LANES - 1
    below = vertical
    centre = (1.0 - 4.0 * diffusion - vertical) + below

    def advance(src, row, f, tile, after):
        rolled = pltpu.roll(tile, LANES - 1, 2)
        right = jnp.where(last, jnp.concatenate([rolled[1:], rolled[:1]], axis=0), rolled)
        rolled = pltpu.roll(tile, 1, 2)
        left = jnp.where(first, jnp.concatenate([rolled[-1:], rolled[:-1]], axis=0), rolled)
        return (
            centre * tile
            + diffusion * (src[f, row + 1] + src[f, row - 1])
            + (diffusion - advection) * right
            + (diffusion + advection) * left
            + pull[f] * after
        )

    def rows_on(src, dst, start, count, edge):
        def body(k, carry):
            row = start + k
            if edge:
                y = sl * R + row - W
                keep = jnp.where((y >= 0) & (y < slabs * R), 1.0, 0.0).astype(F32)
            tile = src[0, row]
            head = tile
            for f in range(F):
                after = src[f + 1, row] if f + 1 < F else head
                new = advance(src, row, f, tile, after)
                dst[f, row] = new * keep if edge else new
                tile = after
            return carry

        lax.fori_loop(0, count, body, 0)

    rows_on(s0, s1, W + 1, R - 2, False)
    rows_on(s1, s2, W + 2, R - 4, False)
    rows_on(s2, s3, W + 3, R - 6, False)

    for side in range(2):
        there = has_low if side == 0 else has_high
        base = 0 if side == 0 else W + R

        @pl.when(there)
        def _():
            for f in range(F):
                pltpu.make_async_remote_copy(
                    src_ref=hs.at[1 - side, f], dst_ref=hr.at[side, f],
                    send_sem=halo_send.at[1 - side, f], recv_sem=halo_recv.at[side, f],
                    device_id=(mu, sl), device_id_type=MESH,
                ).wait_recv()
                for q in range(2):
                    pair = hr[side, f, q].astype(F32)
                    s0[f, base + 2 * q] = pair[:, :M]
                    s0[f, base + 2 * q + 1] = pair[:, M:]

        @pl.when(jnp.logical_not(there))
        def _():
            for f in range(F):
                for k in range(W):
                    s0[f, base + k] = jnp.zeros((T, M, LANES), F32)

    rows_on(s0, s1, 1, 4, True)
    rows_on(s0, s1, 11, 4, True)
    rows_on(s1, s2, 2, 4, True)
    rows_on(s1, s2, 10, 4, True)
    rows_on(s2, s3, 3, 4, True)
    rows_on(s2, s3, 9, 4, True)

    def last_step(q, carry):
        row = W + 2 * q
        tiles = [s3[0, row], s3[0, row + 1]]
        heads = tiles
        for f in range(F):
            afters = [s3[f + 1, row], s3[f + 1, row + 1]] if f + 1 < F else heads
            new = [advance(s3, row + k, f, tiles[k], afters[k]) for k in range(2)]
            xs[f, :, pl.ds(pl.multiple_of(q * 2 * M, 2 * M), 2 * M), :] = jnp.concatenate(new, axis=1).astype(BF16)
            tiles = afters
        return carry

    lax.fori_loop(0, R // 2, last_step, 0)

    for i in range(1, M):
        oc_copy(i).wait()

    def observe(q, carry):
        at = pl.ds(pl.multiple_of(q * 2 * M, 2 * M), 2 * M)
        cells = [jnp.broadcast_to(oc[:, pl.ds(2 * q + k, 1), :], (T, M, LANES)) for k in range(2)]
        cells = jnp.concatenate(cells, axis=1).reshape(T * 2 * M, LANES)
        kind, column = cells // LANES, lax.rem(cells, LANES)
        seen = jnp.zeros((T * 2 * M, LANES), F32)
        for f in range(F):
            tile = xs[f, :, at, :].astype(F32).reshape(T * 2 * M, LANES)
            picked = jnp.take_along_axis(tile, column, axis=1, mode="promise_in_bounds")
            seen = jnp.where(kind == f, picked, seen)
        ys[:, at, :] = seen.reshape(T, 2 * M, LANES).astype(BF16)
        return carry

    lax.fori_loop(0, R // 2, observe, 0)

    def ys_copy(i):
        return pltpu.make_async_remote_copy(
            src_ref=ys.at[others[i]], dst_ref=yr.at[0, mu], send_sem=ys_send.at[i], recv_sem=ys_recv.at[i],
            device_id=(others[i], sl), device_id_type=MESH,
        )

    def xs_copy(f, i):
        return pltpu.make_async_remote_copy(
            src_ref=xs.at[f, others[i]], dst_ref=xr.at[f, mu], send_sem=xs_send.at[f, i], recv_sem=xs_recv.at[f, i],
            device_id=(others[i], sl), device_id_type=MESH,
        )

    for i in range(1, M):
        ys_copy(i).start()
    own_y = pltpu.make_async_copy(ys.at[mu], yr.at[0, mu], own_sem.at[0])
    own_y.start()
    own_x = pltpu.make_async_copy(xs.at[:, mu], xr.at[:, mu], own_sem.at[1])
    own_x.start()
    for f in range(F):
        for i in range(1, M):
            xs_copy(f, i).start()

    def yf_copy(side, i):
        peer = sl - 1 if side == 0 else sl + 1
        origin = lax.rem(mu - i + M, M)
        return pltpu.make_async_remote_copy(
            src_ref=yr.at[0, origin], dst_ref=yr.at[2 - side, origin],
            send_sem=yf_send.at[side, i], recv_sem=yf_recv.at[1 - side, i],
            device_id=(mu, peer), device_id_type=MESH,
        )

    for i in range(M):
        if i == 0:
            own_y.wait()
        else:
            ys_copy(i).wait()

        @pl.when(has_low)
        def _():
            yf_copy(0, i).start()

        @pl.when(has_high)
        def _():
            yf_copy(1, i).start()

    def gram_rows(slot):
        first_row = (R, 0, 2 * R)[slot]

        def body(q, carry):
            at = pl.ds(pl.multiple_of(q * 2 * M, 2 * M), 2 * M)
            pair = yr[slot, :, at, :].astype(F32)
            for k in range(2):
                y = pair[:, k * M : (k + 1) * M, :].reshape(ENS, LANES)
                mean = jnp.sum(y, axis=0, keepdims=True) * (1.0 / ENS)
                pert = y - mean
                prec = pv[slot, 0, pl.ds(2 * q + k, 1), :]
                value = pv[slot, 1, pl.ds(2 * q + k, 1), :]
                weighted = jnp.broadcast_to(prec * (value - mean), (8, LANES))
                left = jnp.concatenate([pert * prec, weighted], axis=0)
                gs[first_row + 2 * q + k] = mm_nt(left, jnp.concatenate([pert, pert], axis=0))
            return carry

        lax.fori_loop(0, R // 2, body, 0)

    gram_rows(0)
    for side in range(2):
        there = has_low if side == 0 else has_high

        @pl.when(there)
        def _():
            pltpu.make_async_remote_copy(
                src_ref=pv.at[0], dst_ref=pv.at[1 + side], send_sem=pv_send.at[1 - side], recv_sem=pv_recv.at[side],
                device_id=(mu, sl), device_id_type=MESH,
            ).wait_recv()
            for i in range(M):
                origin = lax.rem(mu - i + M, M)
                pltpu.make_async_remote_copy(
                    src_ref=yr.at[0, origin], dst_ref=yr.at[1 + side, origin],
                    send_sem=yf_send.at[1 - side, i], recv_sem=yf_recv.at[side, i],
                    device_id=(mu, sl), device_id_type=MESH,
                ).wait_recv()

        @pl.when(jnp.logical_not(there))
        def _():
            yr[1 + side] = jnp.zeros((M, R * M, LANES), BF16)
            pv[1 + side] = jnp.zeros((2, R, LANES), F32)

        gram_rows(1 + side)

    row64 = lax.broadcasted_iota(jnp.int32, (ENS, LANES), 0)
    lane64 = lax.broadcasted_iota(jnp.int32, (ENS, LANES), 1)
    low64 = lane64 < ENS
    eye = jnp.where(lax.rem(lane64, ENS) == row64, 1.0, 0.0).astype(F32)
    y18 = lax.broadcasted_iota(jnp.int32, (24, LANES), 0)
    low18 = lax.broadcasted_iota(jnp.int32, (24, LANES), 1) < ENS
    low1 = low18[:1]

    def both(a):
        return jnp.concatenate([jnp.where(low64, a, 0.0), jnp.where(low64, 0.0, a)], axis=0)

    amats, gvecs, scales = [], [], []
    for p in range(R // 2):
        radius = jnp.where(low18, cut_ref[2 * p], cut_ref[2 * p + 1]).astype(F32)
        away = jnp.abs(y18 - jnp.where(low18, 2 * p + R, 2 * p + 1 + R)).astype(F32)
        weight = jnp.maximum(0.0, 1.0 - away / (radius + 1.0))
        total = jnp.zeros((ENS + 8, LANES), F32)
        for y in range(2 * p, 2 * p + 2 * HALO + 2):
            total = total + weight[y : y + 1] * gs[y]
        amat = (ENS - 1.0) * eye + total[:ENS]
        sums = jnp.sum(amat * amat, axis=0, keepdims=True)
        low = jnp.sum(jnp.where(low1, sums, 0.0), axis=1, keepdims=True)
        high = jnp.sum(jnp.where(low1, 0.0, sums), axis=1, keepdims=True)
        amats.append(amat)
        gvecs.append(total[ENS:])
        scales.append(jnp.sqrt(jnp.where(low1, low, high)))

    ymats = [a / s for a, s in zip(amats, scales)]
    middles = [1.5 * eye - 0.5 * y for y in ymats]
    zmats = middles
    ymats = [mm(y, both(m)) for y, m in zip(ymats, middles)]
    for step_idx in range(1, NS_STEPS):
        middles = [1.5 * eye - 0.5 * mm(z, both(y)) for z, y in zip(zmats, ymats)]
        if step_idx + 1 < NS_STEPS:
            new = [mm(jnp.concatenate([y, z], axis=0), both(m)) for y, z, m in zip(ymats, zmats, middles)]
            ymats, zmats = [n[:ENS] for n in new], [n[ENS:] for n in new]
        else:
            zmats = [mm(m, both(z)) for m, z in zip(middles, zmats)]

    source = lax.broadcasted_iota(jnp.int32, (LANES, LANES), 0)
    target = lax.broadcasted_iota(jnp.int32, (LANES, LANES), 1)
    same_row = source // ENS == lax.rem(target // M, 2)
    same_member = lax.rem(source, ENS) == (target // (2 * M)) * M + lax.rem(target, M)
    spread = jnp.where(same_row, jnp.where(same_member, 1.0 - 1.0 / ENS, -1.0 / ENS), 0.0).astype(BF16)
    odd64 = lax.rem(lane64 // M, 2) == 1
    am[...] = jnp.zeros(am.shape, F32)
    vsum = jnp.zeros((ENS, LANES), F32)
    for p in range(R // 2):
        z, scale = both(zmats[p]), scales[p]
        wbar = mm(mm(gvecs[p], z), z)[:1] / scale
        v = math.sqrt(ENS - 1.0) * zmats[p] / jnp.sqrt(scale) + wbar
        vsum = vsum + v
        vh, vl = split(v)
        a = dot(vh, spread) + dot(vl, spread) + 1.0 / ENS
        am[p, pl.ds(2 * p, ENS, stride=R), :] = jnp.where(odd64, 0.0, a)
        am[p, pl.ds(2 * p + 1, ENS, stride=R), :] = jnp.where(odd64, a, 0.0)

    for i in range(1, M):
        pp_copy(i).wait()
    every = pp[...].reshape(ENS, LANES)
    pbar = jnp.sum(every, axis=0, keepdims=True) * (1.0 / ENS)
    ppert = every - pbar
    ps[...] = mm(vsum, jnp.concatenate([ppert, ppert], axis=0)).reshape(M, M, LANES)

    def ra_copy(i):
        return pltpu.make_async_remote_copy(
            src_ref=ps.at[others[i]], dst_ref=ra.at[mu], send_sem=ra_send.at[i], recv_sem=ra_recv.at[i],
            device_id=(others[i], sl), device_id_type=MESH,
        )

    for i in range(1, M):
        ra_copy(i).start()
    ra[mu] = ps[mu]

    lanes_here = pl.ds(pl.multiple_of(mu * LANES, LANES), LANES)

    def os_copy(f, i):
        return pltpu.make_async_remote_copy(
            src_ref=os_.at[f, others[i]], dst_ref=out_ref.at[:, f, :, lanes_here],
            send_sem=os_send.at[f, i], recv_sem=os_recv.at[f, i],
            device_id=(others[i], sl), device_id_type=MESH,
        )

    def own_copy(f):
        return pltpu.make_async_copy(os_.at[f, mu], out_ref.at[:, f, :, lanes_here], own_sem.at[2 + f])

    own_x.wait()
    for f in range(F):
        for i in range(1, M):
            xs_copy(f, i).wait()
        tiles = [xr[f, :, q * 2 * M : (q + 1) * 2 * M, :].reshape(2 * ENS, LANES) for q in range(R // 2)]
        field = jnp.concatenate(tiles, axis=0)
        for h in range(4):
            ah, al = split(jnp.concatenate([am[p, h * LANES : (h + 1) * LANES, :] for p in range(R // 2)], axis=1))
            new = dot(ah, field) + dot(al, field)
            os_[f, 2 * h : 2 * h + 2] = new.reshape(2, M, R, LANES).astype(BF16)
        for i in range(1, M):
            os_copy(f, i).start()
        own_copy(f).start()

    for i in range(1, M):
        ra_copy(i).wait()
    rb[place] = jnp.sum(ra[...], axis=0)

    def rb_copy(i):
        peer = band * group + lax.rem(place + i, group)
        return pltpu.make_async_remote_copy(
            src_ref=rb.at[place], dst_ref=rb.at[place], send_sem=rb_send.at[i], recv_sem=rb_recv.at[i],
            device_id=(mu, peer), device_id_type=MESH,
        )

    def rc_copy(i):
        peer = lax.rem(sl + i * group, slabs)
        return pltpu.make_async_remote_copy(
            src_ref=rc.at[band], dst_ref=rc.at[band], send_sem=rc_send.at[i], recv_sem=rc_recv.at[i],
            device_id=(mu, peer), device_id_type=MESH,
        )

    for i in range(1, group):
        rb_copy(i).start()
    for i in range(1, group):
        rb_copy(i).wait()
    rc[band] = jnp.sum(rb[...], axis=0)
    for i in range(1, bands):
        rc_copy(i).start()
    for i in range(1, bands):
        rc_copy(i).wait()
    total = jnp.sum(rc[...], axis=0) * (1.0 / (slabs * R * M)) + pbar
    pout_ref[...] = total[:, : pout_ref.shape[1]]

    for f in range(F):
        for i in range(1, M):
            os_copy(f, i).wait()
        own_copy(f).wait()
    for side in range(2):
        there = has_low if side == 0 else has_high

        @pl.when(there)
        def _():
            for f in range(F):
                halo_copy(side, f).wait_send()
            pv_copy(side).wait_send()
            for i in range(M):
                yf_copy(side, i).wait_send()


def local(prior_ensemble_fields, params, influence, obs_cell, obs_value, obs_prec, cutoff):
    slabs = lax.axis_size("slab")
    group = 8 if slabs % 8 == 0 else slabs
    bands = slabs // group
    npar = params.shape[1]
    vmem = pl.BlockSpec(memory_space=pltpu.VMEM)
    dma = pltpu.SemaphoreType.DMA
    ext = R + 2 * W
    analysis, param_analysis = pl.pallas_call(
        lambda *refs: kernel(slabs, group, *refs),
        out_shape=(
            jax.ShapeDtypeStruct((M, F, R, T * LANES), BF16),
            jax.ShapeDtypeStruct((M, npar), F32),
        ),
        in_specs=[
            pl.BlockSpec(memory_space=pl.ANY), vmem, vmem, vmem, vmem, vmem,
            pl.BlockSpec(memory_space=pltpu.SMEM),
        ],
        out_specs=(pl.BlockSpec(memory_space=pl.ANY), vmem),
        scratch_shapes=[
            pltpu.VMEM((F, ext, T, M, LANES), F32),
            pltpu.VMEM((F, ext, T, M, LANES), F32),
            pltpu.VMEM((F, ext, T, M, LANES), F32),
            pltpu.VMEM((F, ext, T, M, LANES), F32),
            pltpu.VMEM((2, F, 2, T, 2 * M, LANES), BF16),
            pltpu.VMEM((2, F, 2, T, 2 * M, LANES), BF16),
            pltpu.VMEM((F, T, R * M, LANES), BF16),
            pltpu.VMEM((F, M, R * M, LANES), BF16),
            pltpu.VMEM((T, R * M, LANES), BF16),
            pltpu.VMEM((3, M, R * M, LANES), BF16),
            pltpu.VMEM((M, R, LANES), jnp.int32),
            pltpu.VMEM((3, 2, R, LANES), F32),
            pltpu.VMEM((M, M, LANES), F32),
            pltpu.VMEM((3 * R, ENS + 8, LANES), F32),
            pltpu.VMEM((R // 2, ENS * R, LANES), F32),
            pltpu.VMEM((F, M, M, R, LANES), BF16),
            pltpu.VMEM((M, M, LANES), F32),
            pltpu.VMEM((M, M, LANES), F32),
            pltpu.VMEM((group, M, LANES), F32),
            pltpu.VMEM((bands, M, LANES), F32),
            dma((F, M)), dma((2, F)), dma((2, F)), dma((2,)), dma((2,)),
            dma((M,)), dma((M,)), dma((M,)), dma((M,)),
            dma((M,)), dma((M,)), dma((2, M)), dma((2, M)), dma((F, M)), dma((F, M)), dma((F, M)), dma((F, M)),
            dma((M,)), dma((M,)), dma((group,)), dma((group,)), dma((bands,)), dma((bands,)), dma((2 + F,)),
        ],
        compiler_params=pltpu.CompilerParams(
            collective_id=0, has_side_effects=True, vmem_limit_bytes=56 * 1024 * 1024
        ),
        name="cycle",
    )(
        prior_ensemble_fields.reshape(M, F, R, T, LANES),
        params,
        influence.T,
        obs_cell.reshape(R, LANES),
        obs_value.reshape(R, LANES),
        obs_prec.reshape(R, LANES),
        cutoff,
    )
    return analysis.reshape(M, F, R, 1, T * LANES), param_analysis


def solution(mesh):
    in_specs = (
        P("member", None, "slab", None, None),
        P("member", None),
        P(),
        P("slab", "member", None),
        P("slab", "member", None),
        P("slab", "member", None),
        P("slab"),
    )
    out_specs = (P("member", None, "slab", None, None), P("member", None))
    return jax.shard_map(local, mesh=mesh, in_specs=in_specs, out_specs=out_specs, check_vma=False)
```

```python
import math

import jax
import jax.numpy as jnp
from jax import lax
from jax.experimental import pallas as pl
from jax.experimental.pallas import tpu as pltpu
from jax.sharding import PartitionSpec as P

STEPS = 4
HALO = 8
EARLY = 3
STAGE_AT = (5, 5)
NS_STEPS = 5
MESH = pl.DeviceIdType.MESH
F32 = jnp.float32
BF16 = jnp.bfloat16

diffusion = 0.2
advection = 0.15
vertical = 0.1
coupling = 0.2

M = 8
F = 6
R = 8
T = 8
LANES = 128
ENS = 64
W = STEPS


def split(a):
    high = a.astype(BF16)
    return high, (a - high.astype(F32)).astype(BF16)


def dot(a, b):
    return jnp.dot(a, b, preferred_element_type=F32)


def dot_nt(a, b):
    return lax.dot_general(a, b, (((1,), (1,)), ((), ())), preferred_element_type=F32)


def mm(left, right):
    lh, ll = split(left)
    rh, rl = split(right)
    return dot(lh, rh) + (dot(lh, rl) + dot(ll, rh))


def mm_nt(left, right):
    lh, ll = split(left)
    rh, rl = split(right)
    return dot_nt(lh, rh) + (dot_nt(lh, rl) + dot_nt(ll, rh))


def kernel(
    slabs,
    group,
    x_ref, params_ref, infl_ref, cell_ref, value_ref, prec_ref, cut_ref,
    out_ref, pout_ref,
    s0, s1, s2, s3, hs, hr, xs, xr, ys, yr, oc, pv, pp, gs, am, os_, ps, ra, rb, rc,
    load_sem, halo_send, halo_recv, pv_send, pv_recv, oc_send, oc_recv, pp_send, pp_recv,
    ys_send, ys_recv, yf_send, yf_recv, xs_send, xs_recv, os_send, os_recv,
    ra_send, ra_recv, rb_send, rb_recv, rc_send, rc_recv, own_sem,
):
    mu = lax.axis_index("member")
    sl = lax.axis_index("slab")
    has_low = sl > 0
    has_high = sl < slabs - 1
    bands = slabs // group
    band, place = sl // group, lax.rem(sl, group)

    loads = []
    for f in range(F):
        for m in range(M):
            copy = pltpu.make_async_copy(
                x_ref.at[m, f], s0.at[f, pl.ds(W, R), :, m, :], load_sem.at[f, m]
            )
            copy.start()
            loads.append(copy)

    barrier = pltpu.get_barrier_semaphore()
    others = [lax.rem(mu + i, M) for i in range(M)]
    for i in range(1, M):
        pl.semaphore_signal(barrier, inc=1, device_id=(others[i], sl), device_id_type=MESH)
    for i in range(1, group):
        peer = band * group + lax.rem(place + i, group)
        pl.semaphore_signal(barrier, inc=1, device_id=(mu, peer), device_id_type=MESH)
    for i in range(1, bands):
        peer = lax.rem(sl + i * group, slabs)
        pl.semaphore_signal(barrier, inc=1, device_id=(mu, peer), device_id_type=MESH)

    @pl.when(has_low)
    def _():
        pl.semaphore_signal(barrier, inc=1, device_id=(mu, sl - 1), device_id_type=MESH)

    @pl.when(has_high)
    def _():
        pl.semaphore_signal(barrier, inc=1, device_id=(mu, sl + 1), device_id_type=MESH)

    expected = (M - 1) + (group - 1) + (bands - 1)
    expected = expected + jnp.where(has_low, 1, 0) + jnp.where(has_high, 1, 0)
    pl.semaphore_wait(barrier, expected)

    def halo_copy(side, f):
        peer = sl - 1 if side == 0 else sl + 1
        return pltpu.make_async_remote_copy(
            src_ref=hs.at[side, f], dst_ref=hr.at[1 - side, f],
            send_sem=halo_send.at[side, f], recv_sem=halo_recv.at[1 - side, f],
            device_id=(mu, peer), device_id_type=MESH,
        )

    for f in range(F):
        for m in range(M):
            loads[f * M + m].wait()
        for side in range(2):
            for q in range(2):
                row = W + 4 * side + 2 * q
                pair = jnp.concatenate([s0[f, row], s0[f, row + 1]], axis=1)
                hs[side, f, q] = pair.astype(BF16)

        @pl.when(has_low)
        def _():
            halo_copy(0, f).start()

        @pl.when(has_high)
        def _():
            halo_copy(1, f).start()

    pp[mu] = jnp.zeros((M, LANES), F32)
    pp[mu, :, : params_ref.shape[1]] = params_ref[...]
    oc[mu] = cell_ref[...]
    pv[0, 0] = prec_ref[...]
    pv[0, 1] = value_ref[...]

    def pp_copy(i):
        return pltpu.make_async_remote_copy(
            src_ref=pp.at[mu], dst_ref=pp.at[mu], send_sem=pp_send.at[i], recv_sem=pp_recv.at[i],
            device_id=(others[i], sl), device_id_type=MESH,
        )

    def oc_copy(i):
        return pltpu.make_async_remote_copy(
            src_ref=oc.at[mu], dst_ref=oc.at[mu], send_sem=oc_send.at[i], recv_sem=oc_recv.at[i],
            device_id=(others[i], sl), device_id_type=MESH,
        )

    def pv_copy(side):
        peer = sl - 1 if side == 0 else sl + 1
        return pltpu.make_async_remote_copy(
            src_ref=pv.at[0], dst_ref=pv.at[2 - side], send_sem=pv_send.at[side], recv_sem=pv_recv.at[1 - side],
            device_id=(mu, peer), device_id_type=MESH,
        )

    for i in range(1, M):
        oc_copy(i).start()
        pp_copy(i).start()

    @pl.when(has_low)
    def _():
        pv_copy(0).start()

    @pl.when(has_high)
    def _():
        pv_copy(1).start()

    coef = lax.dot_general(
        params_ref[...], infl_ref[...].astype(F32), (((1,), (1,)), ((), ())),
        precision=lax.Precision.HIGHEST, preferred_element_type=F32,
    )
    pull = [jnp.broadcast_to(coupling * coef[:, f : f + 1], (M, LANES))[None] for f in range(F)]
    lane = lax.broadcasted_iota(jnp.int32, (T, M, LANES), 2)
    first, last = lane == 0, lane == LANES - 1
    below = vertical
    centre = (1.0 - 4.0 * diffusion - vertical) + below

    def advance(src, row, f, tile, after):
        rolled = pltpu.roll(tile, LANES - 1, 2)
        right = jnp.where(last, jnp.concatenate([rolled[1:], rolled[:1]], axis=0), rolled)
        rolled = pltpu.roll(tile, 1, 2)
        left = jnp.where(first, jnp.concatenate([rolled[-1:], rolled[:-1]], axis=0), rolled)
        return (
            centre * tile
            + diffusion * (src[f, row + 1] + src[f, row - 1])
            + (diffusion - advection) * right
            + (diffusion + advection) * left
            + pull[f] * after
        )

    def rows_on(src, dst, start, count, edge):
        def body(k, carry):
            row = start + k
            if edge:
                y = sl * R + row - W
                keep = jnp.where((y >= 0) & (y < slabs * R), 1.0, 0.0).astype(F32)
            tile = src[0, row]
            head = tile
            for f in range(F):
                after = src[f + 1, row] if f + 1 < F else head
                new = advance(src, row, f, tile, after)
                dst[f, row] = new * keep if edge else new
                tile = after
            return carry

        lax.fori_loop(0, count, body, 0)

    rows_on(s0, s1, W + 1, R - 2, False)
    rows_on(s1, s2, W + 2, R - 4, False)
    rows_on(s2, s3, W + 3, R - 6, False)

    def last_step(q, carry):
        row = W + 2 * q
        tiles = [s3[0, row], s3[0, row + 1]]
        heads = tiles
        for f in range(F):
            afters = [s3[f + 1, row], s3[f + 1, row + 1]] if f + 1 < F else heads
            new = [advance(s3, row + k, f, tiles[k], afters[k]) for k in range(2)]
            xs[f, :, pl.ds(pl.multiple_of(q * 2 * M, 2 * M), 2 * M), :] = jnp.concatenate(new, axis=1).astype(BF16)
            tiles = afters
        return carry


    def observe(q, carry):
        at = pl.ds(pl.multiple_of(q * 2 * M, 2 * M), 2 * M)
        cells = [jnp.broadcast_to(oc[:, pl.ds(2 * q + k, 1), :], (T, M, LANES)) for k in range(2)]
        cells = jnp.concatenate(cells, axis=1).reshape(T * 2 * M, LANES)
        kind, column = cells // LANES, lax.rem(cells, LANES)
        seen = jnp.zeros((T * 2 * M, LANES), F32)
        for f in range(F):
            tile = xs[f, :, at, :].astype(F32).reshape(T * 2 * M, LANES)
            picked = jnp.take_along_axis(tile, column, axis=1, mode="promise_in_bounds")
            seen = jnp.where(kind == f, picked, seen)
        ys[:, at, :] = seen.reshape(T, 2 * M, LANES).astype(BF16)
        return carry

    near = 1 - lax.rem(sl, 2)
    for order in range(2):
        side = near if order == 0 else 1 - near
        there = jnp.where(side == 0, sl, slabs - 1 - sl) > 0
        base = side * (W + R)

        @pl.when(there)
        def _():
            for f in range(F):
                pltpu.make_async_remote_copy(
                    src_ref=hs.at[1 - side, f], dst_ref=hr.at[side, f],
                    send_sem=halo_send.at[1 - side, f], recv_sem=halo_recv.at[side, f],
                    device_id=(mu, sl), device_id_type=MESH,
                ).wait_recv()
                for q in range(2):
                    pair = hr[side, f, q].astype(F32)
                    s0[f, base + 2 * q] = pair[:, :M]
                    s0[f, base + 2 * q + 1] = pair[:, M:]

        @pl.when(jnp.logical_not(there))
        def _():
            for f in range(F):
                for k in range(W):
                    s0[f, base + k] = jnp.zeros((T, M, LANES), F32)

        rows_on(s0, s1, 1 + 10 * side, 4, True)
        rows_on(s1, s2, 2 + 8 * side, 4, True)
        rows_on(s2, s3, 3 + 6 * side, 4, True)
        lax.fori_loop(2 * side, 2 * side + 2, last_step, 0)
        if order == 0:
            for i in range(1, M):
                oc_copy(i).wait()
        lax.fori_loop(2 * side, 2 * side + 2, observe, 0)

    def ys_copy(i):
        return pltpu.make_async_remote_copy(
            src_ref=ys.at[others[i]], dst_ref=yr.at[0, mu], send_sem=ys_send.at[i], recv_sem=ys_recv.at[i],
            device_id=(others[i], sl), device_id_type=MESH,
        )

    def xs_copy(f, i):
        return pltpu.make_async_remote_copy(
            src_ref=xs.at[f, others[i]], dst_ref=xr.at[f, mu], send_sem=xs_send.at[f, i], recv_sem=xs_recv.at[f, i],
            device_id=(others[i], sl), device_id_type=MESH,
        )

    for i in range(1, M):
        ys_copy(i).start()
    own_y = pltpu.make_async_copy(ys.at[mu], yr.at[0, mu], own_sem.at[0])
    own_y.start()
    own_x = pltpu.make_async_copy(xs.at[:, mu], xr.at[:, mu], own_sem.at[1])
    own_x.start()
    for f in range(EARLY):
        for i in range(1, M):
            xs_copy(f, i).start()

    def yf_copy(side, i):
        peer = sl - 1 if side == 0 else sl + 1
        origin = lax.rem(mu - i + M, M)
        return pltpu.make_async_remote_copy(
            src_ref=yr.at[0, origin], dst_ref=yr.at[2 - side, origin],
            send_sem=yf_send.at[side, i], recv_sem=yf_recv.at[1 - side, i],
            device_id=(mu, peer), device_id_type=MESH,
        )

    for i in range(M):
        if i == 0:
            own_y.wait()
        else:
            ys_copy(i).wait()

        @pl.when(has_low)
        def _():
            yf_copy(0, i).start()

        @pl.when(has_high)
        def _():
            yf_copy(1, i).start()

    for f in range(EARLY, F):
        for i in range(1, M):
            xs_copy(f, i).start()

    def gram_rows(slot):
        first_row = (R, 0, 2 * R)[slot]

        def body(q, carry):
            at = pl.ds(pl.multiple_of(q * 2 * M, 2 * M), 2 * M)
            pair = yr[slot, :, at, :].astype(F32)
            for k in range(2):
                y = pair[:, k * M : (k + 1) * M, :].reshape(ENS, LANES)
                mean = jnp.sum(y, axis=0, keepdims=True) * (1.0 / ENS)
                pert = y - mean
                prec = pv[slot, 0, pl.ds(2 * q + k, 1), :]
                value = pv[slot, 1, pl.ds(2 * q + k, 1), :]
                weighted = jnp.broadcast_to(prec * (value - mean), (8, LANES))
                left = jnp.concatenate([pert * prec, weighted], axis=0)
                gs[first_row + 2 * q + k] = mm_nt(left, jnp.concatenate([pert, pert], axis=0))
            return carry

        lax.fori_loop(0, R // 2, body, 0)

    gram_rows(0)
    for side in range(2):
        there = has_low if side == 0 else has_high

        @pl.when(there)
        def _():
            pltpu.make_async_remote_copy(
                src_ref=pv.at[0], dst_ref=pv.at[1 + side], send_sem=pv_send.at[1 - side], recv_sem=pv_recv.at[side],
                device_id=(mu, sl), device_id_type=MESH,
            ).wait_recv()
            for i in range(M):
                origin = lax.rem(mu - i + M, M)
                pltpu.make_async_remote_copy(
                    src_ref=yr.at[0, origin], dst_ref=yr.at[1 + side, origin],
                    send_sem=yf_send.at[1 - side, i], recv_sem=yf_recv.at[side, i],
                    device_id=(mu, sl), device_id_type=MESH,
                ).wait_recv()

        @pl.when(jnp.logical_not(there))
        def _():
            yr[1 + side] = jnp.zeros((M, R * M, LANES), BF16)
            pv[1 + side] = jnp.zeros((2, R, LANES), F32)

        gram_rows(1 + side)

    row64 = lax.broadcasted_iota(jnp.int32, (ENS, LANES), 0)
    lane64 = lax.broadcasted_iota(jnp.int32, (ENS, LANES), 1)
    low64 = lane64 < ENS
    eye = jnp.where(lax.rem(lane64, ENS) == row64, 1.0, 0.0).astype(F32)
    y18 = lax.broadcasted_iota(jnp.int32, (24, LANES), 0)
    low18 = lax.broadcasted_iota(jnp.int32, (24, LANES), 1) < ENS
    low1 = low18[:1]

    def both(a):
        return jnp.concatenate([jnp.where(low64, a, 0.0), jnp.where(low64, 0.0, a)], axis=0)

    amats, gvecs, scales = [], [], []
    for p in range(R // 2):
        radius = jnp.where(low18, cut_ref[2 * p], cut_ref[2 * p + 1]).astype(F32)
        away = jnp.abs(y18 - jnp.where(low18, 2 * p + R, 2 * p + 1 + R)).astype(F32)
        weight = jnp.maximum(0.0, 1.0 - away / (radius + 1.0))
        total = jnp.zeros((ENS + 8, LANES), F32)
        for y in range(2 * p, 2 * p + 2 * HALO + 2):
            total = total + weight[y : y + 1] * gs[y]
        amat = (ENS - 1.0) * eye + total[:ENS]
        sums = jnp.sum(amat * amat, axis=0, keepdims=True)
        low = jnp.sum(jnp.where(low1, sums, 0.0), axis=1, keepdims=True)
        high = jnp.sum(jnp.where(low1, 0.0, sums), axis=1, keepdims=True)
        amats.append(amat)
        gvecs.append(total[ENS:])
        scales.append(jnp.sqrt(jnp.where(low1, low, high)))

    ymats = [a / s for a, s in zip(amats, scales)]
    middles = [1.5 * eye - 0.5 * y for y in ymats]
    zmats = middles
    ymats = [mm(y, both(m)) for y, m in zip(ymats, middles)]
    for step_idx in range(1, NS_STEPS):
        middles = [1.5 * eye - 0.5 * mm(z, both(y)) for z, y in zip(zmats, ymats)]
        if step_idx + 1 < NS_STEPS:
            new = [mm(jnp.concatenate([y, z], axis=0), both(m)) for y, z, m in zip(ymats, zmats, middles)]
            ymats, zmats = [n[:ENS] for n in new], [n[ENS:] for n in new]
        else:
            zmats = [mm(m, both(z)) for m, z in zip(middles, zmats)]

    source = lax.broadcasted_iota(jnp.int32, (LANES, LANES), 0)
    target = lax.broadcasted_iota(jnp.int32, (LANES, LANES), 1)
    same_row = source // ENS == lax.rem(target // M, 2)
    same_member = lax.rem(source, ENS) == (target // (2 * M)) * M + lax.rem(target, M)
    spread = jnp.where(same_row, jnp.where(same_member, 1.0 - 1.0 / ENS, -1.0 / ENS), 0.0).astype(BF16)
    odd64 = lax.rem(lane64 // M, 2) == 1
    am[...] = jnp.zeros(am.shape, F32)
    vsum = jnp.zeros((ENS, LANES), F32)
    for p in range(R // 2):
        z, scale = both(zmats[p]), scales[p]
        wbar = mm(mm(gvecs[p], z), z)[:1] / scale
        v = math.sqrt(ENS - 1.0) * zmats[p] / jnp.sqrt(scale) + wbar
        vsum = vsum + v
        vh, vl = split(v)
        a = dot(vh, spread) + dot(vl, spread) + 1.0 / ENS
        am[p, pl.ds(2 * p, ENS, stride=R), :] = jnp.where(odd64, 0.0, a)
        am[p, pl.ds(2 * p + 1, ENS, stride=R), :] = jnp.where(odd64, a, 0.0)

    for i in range(1, M):
        pp_copy(i).wait()
    every = pp[...].reshape(ENS, LANES)
    pbar = jnp.sum(every, axis=0, keepdims=True) * (1.0 / ENS)
    ppert = every - pbar
    ps[...] = mm(vsum, jnp.concatenate([ppert, ppert], axis=0)).reshape(M, M, LANES)

    def ra_copy(i):
        return pltpu.make_async_remote_copy(
            src_ref=ps.at[others[i]], dst_ref=ra.at[mu], send_sem=ra_send.at[i], recv_sem=ra_recv.at[i],
            device_id=(others[i], sl), device_id_type=MESH,
        )

    for i in range(1, M):
        ra_copy(i).start()
    ra[mu] = ps[mu]

    lanes_here = pl.ds(pl.multiple_of(mu * LANES, LANES), LANES)

    def os_copy(f, i):
        return pltpu.make_async_remote_copy(
            src_ref=os_.at[f, others[i]], dst_ref=out_ref.at[:, f, :, lanes_here],
            send_sem=os_send.at[f, i], recv_sem=os_recv.at[f, i],
            device_id=(others[i], sl), device_id_type=MESH,
        )

    def own_copy(f):
        return pltpu.make_async_copy(os_.at[f, mu], out_ref.at[:, f, :, lanes_here], own_sem.at[2 + f])

    def rb_copy(i):
        peer = band * group + lax.rem(place + i, group)
        return pltpu.make_async_remote_copy(
            src_ref=rb.at[place], dst_ref=rb.at[place], send_sem=rb_send.at[i], recv_sem=rb_recv.at[i],
            device_id=(mu, peer), device_id_type=MESH,
        )

    def rc_copy(i):
        peer = lax.rem(sl + i * group, slabs)
        return pltpu.make_async_remote_copy(
            src_ref=rc.at[band], dst_ref=rc.at[band], send_sem=rc_send.at[i], recv_sem=rc_recv.at[i],
            device_id=(mu, peer), device_id_type=MESH,
        )

    own_x.wait()
    for f in range(F):
        for i in range(1, M):
            xs_copy(f, i).wait()
        tiles = [xr[f, :, q * 2 * M : (q + 1) * 2 * M, :].reshape(2 * ENS, LANES) for q in range(R // 2)]
        field = jnp.concatenate(tiles, axis=0)
        for h in range(4):
            ah, al = split(jnp.concatenate([am[p, h * LANES : (h + 1) * LANES, :] for p in range(R // 2)], axis=1))
            new = dot(ah, field) + dot(al, field)
            os_[f, 2 * h : 2 * h + 2] = new.reshape(2, M, R, LANES).astype(BF16)
        for i in range(1, M):
            os_copy(f, i).start()
        own_copy(f).start()

        if f == STAGE_AT[0]:
            for i in range(1, M):
                ra_copy(i).wait()
            rb[place] = jnp.sum(ra[...], axis=0)
            for i in range(1, group):
                rb_copy(i).start()
        if f == STAGE_AT[1]:
            for i in range(1, group):
                rb_copy(i).wait()
            rc[band] = jnp.sum(rb[...], axis=0)
            for i in range(1, bands):
                rc_copy(i).start()

    for i in range(1, bands):
        rc_copy(i).wait()
    total = jnp.sum(rc[...], axis=0) * (1.0 / (slabs * R * M)) + pbar
    pout_ref[...] = total[:, : pout_ref.shape[1]]

    for f in range(F):
        for i in range(1, M):
            os_copy(f, i).wait()
        own_copy(f).wait()
    for side in range(2):
        there = has_low if side == 0 else has_high

        @pl.when(there)
        def _():
            for f in range(F):
                halo_copy(side, f).wait_send()
            pv_copy(side).wait_send()
            for i in range(M):
                yf_copy(side, i).wait_send()


def local(prior_ensemble_fields, params, influence, obs_cell, obs_value, obs_prec, cutoff):
    slabs = lax.axis_size("slab")
    group = 8 if slabs % 8 == 0 else slabs
    bands = slabs // group
    npar = params.shape[1]
    vmem = pl.BlockSpec(memory_space=pltpu.VMEM)
    dma = pltpu.SemaphoreType.DMA
    ext = R + 2 * W
    analysis, param_analysis = pl.pallas_call(
        lambda *refs: kernel(slabs, group, *refs),
        out_shape=(
            jax.ShapeDtypeStruct((M, F, R, T * LANES), BF16),
            jax.ShapeDtypeStruct((M, npar), F32),
        ),
        in_specs=[
            pl.BlockSpec(memory_space=pl.ANY), vmem, vmem, vmem, vmem, vmem,
            pl.BlockSpec(memory_space=pltpu.SMEM),
        ],
        out_specs=(pl.BlockSpec(memory_space=pl.ANY), vmem),
        scratch_shapes=[
            pltpu.VMEM((F, ext, T, M, LANES), F32),
            pltpu.VMEM((F, ext, T, M, LANES), F32),
            pltpu.VMEM((F, ext, T, M, LANES), F32),
            pltpu.VMEM((F, ext, T, M, LANES), F32),
            pltpu.VMEM((2, F, 2, T, 2 * M, LANES), BF16),
            pltpu.VMEM((2, F, 2, T, 2 * M, LANES), BF16),
            pltpu.VMEM((F, T, R * M, LANES), BF16),
            pltpu.VMEM((F, M, R * M, LANES), BF16),
            pltpu.VMEM((T, R * M, LANES), BF16),
            pltpu.VMEM((3, M, R * M, LANES), BF16),
            pltpu.VMEM((M, R, LANES), jnp.int32),
            pltpu.VMEM((3, 2, R, LANES), F32),
            pltpu.VMEM((M, M, LANES), F32),
            pltpu.VMEM((3 * R, ENS + 8, LANES), F32),
            pltpu.VMEM((R // 2, ENS * R, LANES), F32),
            pltpu.VMEM((F, M, M, R, LANES), BF16),
            pltpu.VMEM((M, M, LANES), F32),
            pltpu.VMEM((M, M, LANES), F32),
            pltpu.VMEM((group, M, LANES), F32),
            pltpu.VMEM((bands, M, LANES), F32),
            dma((F, M)), dma((2, F)), dma((2, F)), dma((2,)), dma((2,)),
            dma((M,)), dma((M,)), dma((M,)), dma((M,)),
            dma((M,)), dma((M,)), dma((2, M)), dma((2, M)), dma((F, M)), dma((F, M)), dma((F, M)), dma((F, M)),
            dma((M,)), dma((M,)), dma((group,)), dma((group,)), dma((bands,)), dma((bands,)), dma((2 + F,)),
        ],
        compiler_params=pltpu.CompilerParams(
            collective_id=0, has_side_effects=True, vmem_limit_bytes=56 * 1024 * 1024
        ),
        name="cycle",
    )(
        prior_ensemble_fields.reshape(M, F, R, T, LANES),
        params,
        influence.T,
        obs_cell.reshape(R, LANES),
        obs_value.reshape(R, LANES),
        obs_prec.reshape(R, LANES),
        cutoff,
    )
    return analysis.reshape(M, F, R, 1, T * LANES), param_analysis


def solution(mesh):
    in_specs = (
        P("member", None, "slab", None, None),
        P("member", None),
        P(),
        P("slab", "member", None),
        P("slab", "member", None),
        P("slab", "member", None),
        P("slab"),
    )
    out_specs = (P("member", None, "slab", None, None), P("member", None))
    return jax.shard_map(local, mesh=mesh, in_specs=in_specs, out_specs=out_specs, check_vma=False)
```

```python
import math

import jax
import jax.numpy as jnp
from jax import lax
from jax.experimental import pallas as pl
from jax.experimental.pallas import tpu as pltpu
from jax.sharding import PartitionSpec as P

STEPS = 4
HALO = 8
GROUP = 3
STAGE_AT = (4, 5)
NS_STEPS = 5
MESH = pl.DeviceIdType.MESH
F32 = jnp.float32
BF16 = jnp.bfloat16

diffusion = 0.2
advection = 0.15
vertical = 0.1
coupling = 0.2

M = 8
F = 6
R = 8
T = 8
LANES = 128
ENS = 64
W = STEPS


def split(a):
    high = a.astype(BF16)
    return high, (a - high.astype(F32)).astype(BF16)


def dot(a, b):
    return jnp.dot(a, b, preferred_element_type=F32)


def dot_nt(a, b):
    return lax.dot_general(a, b, (((1,), (1,)), ((), ())), preferred_element_type=F32)


def mm(left, right):
    lh, ll = split(left)
    rh, rl = split(right)
    return dot(lh, rh) + (dot(lh, rl) + dot(ll, rh))


def mm_nt(left, right):
    lh, ll = split(left)
    rh, rl = split(right)
    return dot_nt(lh, rh) + (dot_nt(lh, rl) + dot_nt(ll, rh))


def kernel(
    slabs,
    group,
    x_ref, params_ref, infl_ref, cell_ref, value_ref, prec_ref, cut_ref,
    out_ref, pout_ref,
    s0, s1, s2, s3, hs, hr, xs, xr, ys, yr, oc, pv, pp, gs, am, os_, ps, ra, rb, rc,
    load_sem, halo_send, halo_recv, pv_send, pv_recv, oc_send, oc_recv, pp_send, pp_recv,
    ys_send, ys_recv, yf_send, yf_recv, xs_send, xs_recv, os_send, os_recv,
    ra_send, ra_recv, rb_send, rb_recv, rc_send, rc_recv, own_sem,
):
    mu = lax.axis_index("member")
    sl = lax.axis_index("slab")
    has_low = sl > 0
    has_high = sl < slabs - 1
    bands = slabs // group
    band, place = sl // group, lax.rem(sl, group)

    barrier = pltpu.get_barrier_semaphore()
    others = [lax.rem(mu + i, M) for i in range(M)]
    for i in range(1, M):
        pl.semaphore_signal(barrier, inc=1, device_id=(others[i], sl), device_id_type=MESH)
    for i in range(1, group):
        peer = band * group + lax.rem(place + i, group)
        pl.semaphore_signal(barrier, inc=1, device_id=(mu, peer), device_id_type=MESH)
    for i in range(1, bands):
        peer = lax.rem(sl + i * group, slabs)
        pl.semaphore_signal(barrier, inc=1, device_id=(mu, peer), device_id_type=MESH)

    @pl.when(has_low)
    def _():
        pl.semaphore_signal(barrier, inc=1, device_id=(mu, sl - 1), device_id_type=MESH)

    @pl.when(has_high)
    def _():
        pl.semaphore_signal(barrier, inc=1, device_id=(mu, sl + 1), device_id_type=MESH)

    expected = (M - 1) + (group - 1) + (bands - 1)
    expected = expected + jnp.where(has_low, 1, 0) + jnp.where(has_high, 1, 0)

    loads = []
    for f in range(F):
        for m in range(M):
            copy = pltpu.make_async_copy(
                x_ref.at[m, f], s0.at[f, pl.ds(W, R), :, m, :], load_sem.at[f, m]
            )
            copy.start()
            loads.append(copy)

    def halo_copy(side, f):
        peer = sl - 1 if side == 0 else sl + 1
        return pltpu.make_async_remote_copy(
            src_ref=hs.at[side, f], dst_ref=hr.at[1 - side, f],
            send_sem=halo_send.at[side, f], recv_sem=halo_recv.at[1 - side, f],
            device_id=(mu, peer), device_id_type=MESH,
        )

    for f in range(F):
        for m in range(M):
            loads[f * M + m].wait()
        for side in range(2):
            for q in range(2):
                row = W + 4 * side + 2 * q
                pair = jnp.concatenate([s0[f, row], s0[f, row + 1]], axis=1)
                hs[side, f, q] = pair.astype(BF16)

    pl.semaphore_wait(barrier, expected)

    for f in range(F):
        @pl.when(has_low)
        def _():
            halo_copy(0, f).start()

        @pl.when(has_high)
        def _():
            halo_copy(1, f).start()

    pp[mu] = jnp.zeros((M, LANES), F32)
    pp[mu, :, : params_ref.shape[1]] = params_ref[...]
    oc[mu] = cell_ref[...]
    pv[0, 0] = prec_ref[...]
    pv[0, 1] = value_ref[...]

    def pp_copy(i):
        return pltpu.make_async_remote_copy(
            src_ref=pp.at[mu], dst_ref=pp.at[mu], send_sem=pp_send.at[i], recv_sem=pp_recv.at[i],
            device_id=(others[i], sl), device_id_type=MESH,
        )

    def oc_copy(i):
        return pltpu.make_async_remote_copy(
            src_ref=oc.at[mu], dst_ref=oc.at[mu], send_sem=oc_send.at[i], recv_sem=oc_recv.at[i],
            device_id=(others[i], sl), device_id_type=MESH,
        )

    def pv_copy(side):
        peer = sl - 1 if side == 0 else sl + 1
        return pltpu.make_async_remote_copy(
            src_ref=pv.at[0], dst_ref=pv.at[2 - side], send_sem=pv_send.at[side], recv_sem=pv_recv.at[1 - side],
            device_id=(mu, peer), device_id_type=MESH,
        )

    for i in range(1, M):
        oc_copy(i).start()
        pp_copy(i).start()

    @pl.when(has_low)
    def _():
        pv_copy(0).start()

    @pl.when(has_high)
    def _():
        pv_copy(1).start()

    coef = lax.dot_general(
        params_ref[...], infl_ref[...].astype(F32), (((1,), (1,)), ((), ())),
        precision=lax.Precision.HIGHEST, preferred_element_type=F32,
    )
    pull = [jnp.broadcast_to(coupling * coef[:, f : f + 1], (M, LANES))[None] for f in range(F)]
    lane = lax.broadcasted_iota(jnp.int32, (T, M, LANES), 2)
    first, last = lane == 0, lane == LANES - 1
    below = vertical
    centre = (1.0 - 4.0 * diffusion - vertical) + below

    def advance(src, row, f, tile, after):
        rolled = pltpu.roll(tile, LANES - 1, 2)
        right = jnp.where(last, jnp.concatenate([rolled[1:], rolled[:1]], axis=0), rolled)
        rolled = pltpu.roll(tile, 1, 2)
        left = jnp.where(first, jnp.concatenate([rolled[-1:], rolled[:-1]], axis=0), rolled)
        return (
            centre * tile
            + diffusion * (src[f, row + 1] + src[f, row - 1])
            + (diffusion - advection) * right
            + (diffusion + advection) * left
            + pull[f] * after
        )

    def rows_on(src, dst, start, count, edge):
        def body(k, carry):
            row = start + k
            if edge:
                y = sl * R + row - W
                keep = jnp.where((y >= 0) & (y < slabs * R), 1.0, 0.0).astype(F32)
            tile = src[0, row]
            head = tile
            for f in range(F):
                after = src[f + 1, row] if f + 1 < F else head
                new = advance(src, row, f, tile, after)
                dst[f, row] = new * keep if edge else new
                tile = after
            return carry

        lax.fori_loop(0, count, body, 0)

    rows_on(s0, s1, W + 1, R - 2, False)
    rows_on(s1, s2, W + 2, R - 4, False)
    rows_on(s2, s3, W + 3, R - 6, False)

    def last_step(q, carry):
        row = W + 2 * q
        tiles = [s3[0, row], s3[0, row + 1]]
        heads = tiles
        for f in range(F):
            afters = [s3[f + 1, row], s3[f + 1, row + 1]] if f + 1 < F else heads
            new = [advance(s3, row + k, f, tiles[k], afters[k]) for k in range(2)]
            xs[f, :, pl.ds(pl.multiple_of(q * 2 * M, 2 * M), 2 * M), :] = jnp.concatenate(new, axis=1).astype(BF16)
            tiles = afters
        return carry


    def observe(q, carry):
        at = pl.ds(pl.multiple_of(q * 2 * M, 2 * M), 2 * M)
        cells = [jnp.broadcast_to(oc[:, pl.ds(2 * q + k, 1), :], (T, M, LANES)) for k in range(2)]
        cells = jnp.concatenate(cells, axis=1).reshape(T * 2 * M, LANES)
        kind, column = cells // LANES, lax.rem(cells, LANES)
        seen = jnp.zeros((T * 2 * M, LANES), F32)
        for f in range(F):
            tile = xs[f, :, at, :].astype(F32).reshape(T * 2 * M, LANES)
            picked = jnp.take_along_axis(tile, column, axis=1, mode="promise_in_bounds")
            seen = jnp.where(kind == f, picked, seen)
        ys[:, at, :] = seen.reshape(T, 2 * M, LANES).astype(BF16)
        return carry

    near = 1 - lax.rem(sl, 2)
    for order in range(2):
        side = near if order == 0 else 1 - near
        there = jnp.where(side == 0, sl, slabs - 1 - sl) > 0
        base = side * (W + R)

        @pl.when(there)
        def _():
            for f in range(F):
                pltpu.make_async_remote_copy(
                    src_ref=hs.at[1 - side, f], dst_ref=hr.at[side, f],
                    send_sem=halo_send.at[1 - side, f], recv_sem=halo_recv.at[side, f],
                    device_id=(mu, sl), device_id_type=MESH,
                ).wait_recv()
                for q in range(2):
                    pair = hr[side, f, q].astype(F32)
                    s0[f, base + 2 * q] = pair[:, :M]
                    s0[f, base + 2 * q + 1] = pair[:, M:]

        @pl.when(jnp.logical_not(there))
        def _():
            for f in range(F):
                for k in range(W):
                    s0[f, base + k] = jnp.zeros((T, M, LANES), F32)

        rows_on(s0, s1, 1 + 10 * side, 4, True)
        rows_on(s1, s2, 2 + 8 * side, 4, True)
        rows_on(s2, s3, 3 + 6 * side, 4, True)
        lax.fori_loop(2 * side, 2 * side + 2, last_step, 0)
        if order == 0:
            for i in range(1, M):
                oc_copy(i).wait()
        lax.fori_loop(2 * side, 2 * side + 2, observe, 0)

    def ys_copy(i):
        return pltpu.make_async_remote_copy(
            src_ref=ys.at[others[i]], dst_ref=yr.at[0, mu], send_sem=ys_send.at[i], recv_sem=ys_recv.at[i],
            device_id=(others[i], sl), device_id_type=MESH,
        )

    def xs_copy(f, i):
        fields = pl.ds(f, GROUP)
        return pltpu.make_async_remote_copy(
            src_ref=xs.at[fields, others[i]], dst_ref=xr.at[fields, mu], send_sem=xs_send.at[f, i], recv_sem=xs_recv.at[f, i],
            device_id=(others[i], sl), device_id_type=MESH,
        )

    for i in range(1, M):
        ys_copy(i).start()
    own_y = pltpu.make_async_copy(ys.at[mu], yr.at[0, mu], own_sem.at[0])
    own_y.start()
    own_x = pltpu.make_async_copy(xs.at[:, mu], xr.at[:, mu], own_sem.at[1])
    own_x.start()
    for i in range(1, M):
        xs_copy(0, i).start()

    def yf_copy(side, i):
        peer = sl - 1 if side == 0 else sl + 1
        origin = lax.rem(mu - i + M, M)
        return pltpu.make_async_remote_copy(
            src_ref=yr.at[0, origin], dst_ref=yr.at[2 - side, origin],
            send_sem=yf_send.at[side, i], recv_sem=yf_recv.at[1 - side, i],
            device_id=(mu, peer), device_id_type=MESH,
        )

    for i in range(M):
        if i == 0:
            own_y.wait()
        else:
            ys_copy(i).wait()

        @pl.when(has_low)
        def _():
            yf_copy(0, i).start()

        @pl.when(has_high)
        def _():
            yf_copy(1, i).start()

    for f in range(GROUP, F, GROUP):
        for i in range(1, M):
            xs_copy(f, i).start()

    def gram_rows(slot):
        first_row = (R, 0, 2 * R)[slot]

        def body(q, carry):
            at = pl.ds(pl.multiple_of(q * 2 * M, 2 * M), 2 * M)
            pair = yr[slot, :, at, :].astype(F32)
            for k in range(2):
                y = pair[:, k * M : (k + 1) * M, :].reshape(ENS, LANES)
                mean = jnp.sum(y, axis=0, keepdims=True) * (1.0 / ENS)
                pert = y - mean
                prec = pv[slot, 0, pl.ds(2 * q + k, 1), :]
                value = pv[slot, 1, pl.ds(2 * q + k, 1), :]
                weighted = jnp.broadcast_to(prec * (value - mean), (8, LANES))
                left = jnp.concatenate([pert * prec, weighted], axis=0)
                gs[first_row + 2 * q + k] = mm_nt(left, jnp.concatenate([pert, pert], axis=0))
            return carry

        lax.fori_loop(0, R // 2, body, 0)

    gram_rows(0)
    for side in range(2):
        there = has_low if side == 0 else has_high

        @pl.when(there)
        def _():
            pltpu.make_async_remote_copy(
                src_ref=pv.at[0], dst_ref=pv.at[1 + side], send_sem=pv_send.at[1 - side], recv_sem=pv_recv.at[side],
                device_id=(mu, sl), device_id_type=MESH,
            ).wait_recv()
            for i in range(M):
                origin = lax.rem(mu - i + M, M)
                pltpu.make_async_remote_copy(
                    src_ref=yr.at[0, origin], dst_ref=yr.at[1 + side, origin],
                    send_sem=yf_send.at[1 - side, i], recv_sem=yf_recv.at[side, i],
                    device_id=(mu, sl), device_id_type=MESH,
                ).wait_recv()

        @pl.when(jnp.logical_not(there))
        def _():
            yr[1 + side] = jnp.zeros((M, R * M, LANES), BF16)
            pv[1 + side] = jnp.zeros((2, R, LANES), F32)

        gram_rows(1 + side)

    row64 = lax.broadcasted_iota(jnp.int32, (ENS, LANES), 0)
    lane64 = lax.broadcasted_iota(jnp.int32, (ENS, LANES), 1)
    low64 = lane64 < ENS
    eye = jnp.where(lax.rem(lane64, ENS) == row64, 1.0, 0.0).astype(F32)
    y18 = lax.broadcasted_iota(jnp.int32, (24, LANES), 0)
    low18 = lax.broadcasted_iota(jnp.int32, (24, LANES), 1) < ENS
    low1 = low18[:1]

    def both(a):
        return jnp.concatenate([jnp.where(low64, a, 0.0), jnp.where(low64, 0.0, a)], axis=0)

    amats, gvecs, scales = [], [], []
    for p in range(R // 2):
        radius = jnp.where(low18, cut_ref[2 * p], cut_ref[2 * p + 1]).astype(F32)
        away = jnp.abs(y18 - jnp.where(low18, 2 * p + R, 2 * p + 1 + R)).astype(F32)
        weight = jnp.maximum(0.0, 1.0 - away / (radius + 1.0))
        total = jnp.zeros((ENS + 8, LANES), F32)
        for y in range(2 * p, 2 * p + 2 * HALO + 2):
            total = total + weight[y : y + 1] * gs[y]
        amat = (ENS - 1.0) * eye + total[:ENS]
        sums = jnp.sum(amat * amat, axis=0, keepdims=True)
        low = jnp.sum(jnp.where(low1, sums, 0.0), axis=1, keepdims=True)
        high = jnp.sum(jnp.where(low1, 0.0, sums), axis=1, keepdims=True)
        amats.append(amat)
        gvecs.append(total[ENS:])
        scales.append(jnp.sqrt(jnp.where(low1, low, high)))

    ymats = [a / s for a, s in zip(amats, scales)]
    middles = [1.5 * eye - 0.5 * y for y in ymats]
    zmats = middles
    ymats = [mm(y, both(m)) for y, m in zip(ymats, middles)]
    for step_idx in range(1, NS_STEPS):
        middles = [1.5 * eye - 0.5 * mm(z, both(y)) for z, y in zip(zmats, ymats)]
        if step_idx + 1 < NS_STEPS:
            new = [mm(jnp.concatenate([y, z], axis=0), both(m)) for y, z, m in zip(ymats, zmats, middles)]
            ymats, zmats = [n[:ENS] for n in new], [n[ENS:] for n in new]
        else:
            zmats = [mm(m, both(z)) for m, z in zip(middles, zmats)]

    source = lax.broadcasted_iota(jnp.int32, (LANES, LANES), 0)
    target = lax.broadcasted_iota(jnp.int32, (LANES, LANES), 1)
    same_row = source // ENS == lax.rem(target // M, 2)
    same_member = lax.rem(source, ENS) == (target // (2 * M)) * M + lax.rem(target, M)
    spread = jnp.where(same_row, jnp.where(same_member, 1.0 - 1.0 / ENS, -1.0 / ENS), 0.0).astype(BF16)
    odd64 = lax.rem(lane64 // M, 2) == 1
    am[...] = jnp.zeros(am.shape, F32)
    vsum = jnp.zeros((ENS, LANES), F32)
    for p in range(R // 2):
        z, scale = both(zmats[p]), scales[p]
        wbar = mm(mm(gvecs[p], z), z)[:1] / scale
        v = math.sqrt(ENS - 1.0) * zmats[p] / jnp.sqrt(scale) + wbar
        vsum = vsum + v
        vh, vl = split(v)
        a = dot(vh, spread) + dot(vl, spread) + 1.0 / ENS
        am[p, pl.ds(2 * p, ENS, stride=R), :] = jnp.where(odd64, 0.0, a)
        am[p, pl.ds(2 * p + 1, ENS, stride=R), :] = jnp.where(odd64, a, 0.0)

    for i in range(1, M):
        pp_copy(i).wait()
    every = pp[...].reshape(ENS, LANES)
    pbar = jnp.sum(every, axis=0, keepdims=True) * (1.0 / ENS)
    ppert = every - pbar
    ps[...] = mm(vsum, jnp.concatenate([ppert, ppert], axis=0)).reshape(M, M, LANES)

    def ra_copy(i):
        return pltpu.make_async_remote_copy(
            src_ref=ps.at[others[i]], dst_ref=ra.at[mu], send_sem=ra_send.at[i], recv_sem=ra_recv.at[i],
            device_id=(others[i], sl), device_id_type=MESH,
        )

    for i in range(1, M):
        ra_copy(i).start()
    ra[mu] = ps[mu]

    lanes_here = pl.ds(pl.multiple_of(mu * LANES, LANES), LANES)

    def os_copy(f, i):
        return pltpu.make_async_remote_copy(
            src_ref=os_.at[f, others[i]], dst_ref=out_ref.at[:, f, :, lanes_here],
            send_sem=os_send.at[f, i], recv_sem=os_recv.at[f, i],
            device_id=(others[i], sl), device_id_type=MESH,
        )

    def own_copy(f):
        return pltpu.make_async_copy(os_.at[f, mu], out_ref.at[:, f, :, lanes_here], own_sem.at[2 + f])

    def rb_copy(i):
        peer = band * group + lax.rem(place + i, group)
        return pltpu.make_async_remote_copy(
            src_ref=rb.at[place], dst_ref=rb.at[place], send_sem=rb_send.at[i], recv_sem=rb_recv.at[i],
            device_id=(mu, peer), device_id_type=MESH,
        )

    def rc_copy(i):
        peer = lax.rem(sl + i * group, slabs)
        return pltpu.make_async_remote_copy(
            src_ref=rc.at[band], dst_ref=rc.at[band], send_sem=rc_send.at[i], recv_sem=rc_recv.at[i],
            device_id=(mu, peer), device_id_type=MESH,
        )

    own_x.wait()
    for f in range(F):
        if f % GROUP == 0:
            for i in range(1, M):
                xs_copy(f, i).wait()
        tiles = [xr[f, :, q * 2 * M : (q + 1) * 2 * M, :].reshape(2 * ENS, LANES) for q in range(R // 2)]
        field = jnp.concatenate(tiles, axis=0)
        for h in range(4):
            ah, al = split(jnp.concatenate([am[p, h * LANES : (h + 1) * LANES, :] for p in range(R // 2)], axis=1))
            new = dot(ah, field) + dot(al, field)
            os_[f, 2 * h : 2 * h + 2] = new.reshape(2, M, R, LANES).astype(BF16)
        for i in range(1, M):
            os_copy(f, i).start()
        own_copy(f).start()

        if f == STAGE_AT[0]:
            for i in range(1, M):
                ra_copy(i).wait()
            rb[place] = jnp.sum(ra[...], axis=0)
            for i in range(1, group):
                rb_copy(i).start()
        if f == STAGE_AT[1]:
            for i in range(1, group):
                rb_copy(i).wait()
            rc[band] = jnp.sum(rb[...], axis=0)
            for i in range(1, bands):
                rc_copy(i).start()

    for i in range(1, bands):
        rc_copy(i).wait()
    total = jnp.sum(rc[...], axis=0) * (1.0 / (slabs * R * M)) + pbar
    pout_ref[...] = total[:, : pout_ref.shape[1]]

    for f in range(F):
        for i in range(1, M):
            os_copy(f, i).wait()
        own_copy(f).wait()
    for side in range(2):
        there = has_low if side == 0 else has_high

        @pl.when(there)
        def _():
            for f in range(F):
                halo_copy(side, f).wait_send()
            pv_copy(side).wait_send()
            for i in range(M):
                yf_copy(side, i).wait_send()


def local(prior_ensemble_fields, params, influence, obs_cell, obs_value, obs_prec, cutoff):
    slabs = lax.axis_size("slab")
    group = 8 if slabs % 8 == 0 else slabs
    bands = slabs // group
    npar = params.shape[1]
    vmem = pl.BlockSpec(memory_space=pltpu.VMEM)
    dma = pltpu.SemaphoreType.DMA
    ext = R + 2 * W
    analysis, param_analysis = pl.pallas_call(
        lambda *refs: kernel(slabs, group, *refs),
        out_shape=(
            pltpu.VMEM((M, F, R, T * LANES), BF16),
            pltpu.VMEM((M, npar), F32),
        ),
        in_specs=[
            pl.BlockSpec(memory_space=pl.ANY), vmem, vmem, vmem, vmem, vmem,
            pl.BlockSpec(memory_space=pltpu.SMEM),
        ],
        out_specs=(vmem, vmem),
        scratch_shapes=[
            pltpu.VMEM((F, ext, T, M, LANES), F32),
            pltpu.VMEM((F, ext, T, M, LANES), F32),
            pltpu.VMEM((F, ext, T, M, LANES), F32),
            pltpu.VMEM((F, ext, T, M, LANES), F32),
            pltpu.VMEM((2, F, 2, T, 2 * M, LANES), BF16),
            pltpu.VMEM((2, F, 2, T, 2 * M, LANES), BF16),
            pltpu.VMEM((F, T, R * M, LANES), BF16),
            pltpu.VMEM((F, M, R * M, LANES), BF16),
            pltpu.VMEM((T, R * M, LANES), BF16),
            pltpu.VMEM((3, M, R * M, LANES), BF16),
            pltpu.VMEM((M, R, LANES), jnp.int32),
            pltpu.VMEM((3, 2, R, LANES), F32),
            pltpu.VMEM((M, M, LANES), F32),
            pltpu.VMEM((3 * R, ENS + 8, LANES), F32),
            pltpu.VMEM((R // 2, ENS * R, LANES), F32),
            pltpu.VMEM((F, M, M, R, LANES), BF16),
            pltpu.VMEM((M, M, LANES), F32),
            pltpu.VMEM((M, M, LANES), F32),
            pltpu.VMEM((group, M, LANES), F32),
            pltpu.VMEM((bands, M, LANES), F32),
            dma((F, M)), dma((2, F)), dma((2, F)), dma((2,)), dma((2,)),
            dma((M,)), dma((M,)), dma((M,)), dma((M,)),
            dma((M,)), dma((M,)), dma((2, M)), dma((2, M)), dma((F, M)), dma((F, M)), dma((F, M)), dma((F, M)),
            dma((M,)), dma((M,)), dma((group,)), dma((group,)), dma((bands,)), dma((bands,)), dma((2 + F,)),
        ],
        compiler_params=pltpu.CompilerParams(
            collective_id=0, has_side_effects=True, vmem_limit_bytes=56 * 1024 * 1024
        ),
        name="cycle",
    )(
        prior_ensemble_fields.reshape(M, F, R, T, LANES),
        params,
        influence.T,
        obs_cell.reshape(R, LANES),
        obs_value.reshape(R, LANES),
        obs_prec.reshape(R, LANES),
        cutoff,
    )
    return analysis.reshape(M, F, R, 1, T * LANES), param_analysis


def solution(mesh):
    in_specs = (
        P("member", None, "slab", None, None),
        P("member", None),
        P(),
        P("slab", "member", None),
        P("slab", "member", None),
        P("slab", "member", None),
        P("slab"),
    )
    out_specs = (P("member", None, "slab", None, None), P("member", None))
    return jax.shard_map(local, mesh=mesh, in_specs=in_specs, out_specs=out_specs, check_vma=False)
```

```python
import math

import jax
import jax.numpy as jnp
from jax import lax
from jax.experimental import pallas as pl
from jax.experimental.pallas import tpu as pltpu
from jax.sharding import PartitionSpec as P

STEPS = 4
HALO = 8
GROUP = 3
STAGE_AT = (4, 5)
NS_STEPS = 5
MESH = pl.DeviceIdType.MESH
F32 = jnp.float32
BF16 = jnp.bfloat16

diffusion = 0.2
advection = 0.15
vertical = 0.1
coupling = 0.2

M = 8
F = 6
R = 8
T = 8
LANES = 128
ENS = 64
W = STEPS


def split(a):
    high = a.astype(BF16)
    return high, (a - high.astype(F32)).astype(BF16)


def dot(a, b):
    return jnp.dot(a, b, preferred_element_type=F32)


def dot_nt(a, b):
    return lax.dot_general(a, b, (((1,), (1,)), ((), ())), preferred_element_type=F32)


def mm(left, right):
    lh, ll = split(left)
    rh, rl = split(right)
    return dot(lh, rh) + (dot(lh, rl) + dot(ll, rh))


def mm_nt(left, right):
    lh, ll = split(left)
    rh, rl = split(right)
    return dot_nt(lh, rh) + (dot_nt(lh, rl) + dot_nt(ll, rh))


def kernel(
    slabs,
    group,
    x_ref, params_ref, infl_ref, cell_ref, value_ref, prec_ref, cut_ref,
    out_ref, pout_ref,
    s0, s1, s2, s3, hs, hr, xs, xr, ys, yr, oc, pv, pp, gs, am, os_, ps, ra, rb, rc,
    load_sem, halo_send, halo_recv, pv_send, pv_recv, oc_send, oc_recv, pp_send, pp_recv,
    ys_send, ys_recv, yf_send, yf_recv, xs_send, xs_recv, os_send, os_recv,
    ra_send, ra_recv, rb_send, rb_recv, rc_send, rc_recv, own_sem,
):
    mu = lax.axis_index("member")
    sl = lax.axis_index("slab")
    has_low = sl > 0
    has_high = sl < slabs - 1
    bands = slabs // group
    band, place = sl // group, lax.rem(sl, group)

    barrier = pltpu.get_barrier_semaphore()
    others = [lax.rem(mu + i, M) for i in range(M)]
    for i in range(1, M):
        pl.semaphore_signal(barrier, inc=1, device_id=(others[i], sl), device_id_type=MESH)
    for i in range(1, group):
        peer = band * group + lax.rem(place + i, group)
        pl.semaphore_signal(barrier, inc=1, device_id=(mu, peer), device_id_type=MESH)
    for i in range(1, bands):
        peer = lax.rem(sl + i * group, slabs)
        pl.semaphore_signal(barrier, inc=1, device_id=(mu, peer), device_id_type=MESH)

    @pl.when(has_low)
    def _():
        pl.semaphore_signal(barrier, inc=1, device_id=(mu, sl - 1), device_id_type=MESH)

    @pl.when(has_high)
    def _():
        pl.semaphore_signal(barrier, inc=1, device_id=(mu, sl + 1), device_id_type=MESH)

    expected = (M - 1) + (group - 1) + (bands - 1)
    expected = expected + jnp.where(has_low, 1, 0) + jnp.where(has_high, 1, 0)

    loads = []
    for f in range(F):
        for m in range(M):
            copy = pltpu.make_async_copy(
                x_ref.at[m, f], s0.at[f, pl.ds(W, R), :, m, :], load_sem.at[f, m]
            )
            copy.start()
            loads.append(copy)

    def halo_copy(side, f):
        peer = sl - 1 if side == 0 else sl + 1
        return pltpu.make_async_remote_copy(
            src_ref=hs.at[side, f], dst_ref=hr.at[1 - side, f],
            send_sem=halo_send.at[side, f], recv_sem=halo_recv.at[1 - side, f],
            device_id=(mu, peer), device_id_type=MESH,
        )

    for f in range(F):
        for m in range(M):
            loads[f * M + m].wait()
        for side in range(2):
            for q in range(2):
                row = W + 4 * side + 2 * q
                pair = jnp.concatenate([s0[f, row], s0[f, row + 1]], axis=1)
                hs[side, f, q] = pair.astype(BF16)

    am[...] = jnp.zeros(am.shape, F32)

    pl.semaphore_wait(barrier, expected)

    for f in range(F):
        @pl.when(has_low)
        def _():
            halo_copy(0, f).start()

        @pl.when(has_high)
        def _():
            halo_copy(1, f).start()

    pp[mu] = jnp.zeros((M, LANES), F32)
    pp[mu, :, : params_ref.shape[1]] = params_ref[...]
    oc[mu] = cell_ref[...]
    pv[0, 0] = prec_ref[...]
    pv[0, 1] = value_ref[...]

    def pp_copy(i):
        return pltpu.make_async_remote_copy(
            src_ref=pp.at[mu], dst_ref=pp.at[mu], send_sem=pp_send.at[i], recv_sem=pp_recv.at[i],
            device_id=(others[i], sl), device_id_type=MESH,
        )

    def oc_copy(i):
        return pltpu.make_async_remote_copy(
            src_ref=oc.at[mu], dst_ref=oc.at[mu], send_sem=oc_send.at[i], recv_sem=oc_recv.at[i],
            device_id=(others[i], sl), device_id_type=MESH,
        )

    def pv_copy(side):
        peer = sl - 1 if side == 0 else sl + 1
        return pltpu.make_async_remote_copy(
            src_ref=pv.at[0], dst_ref=pv.at[2 - side], send_sem=pv_send.at[side], recv_sem=pv_recv.at[1 - side],
            device_id=(mu, peer), device_id_type=MESH,
        )

    for i in range(1, M):
        oc_copy(i).start()
        pp_copy(i).start()

    @pl.when(has_low)
    def _():
        pv_copy(0).start()

    @pl.when(has_high)
    def _():
        pv_copy(1).start()

    coef = lax.dot_general(
        params_ref[...], infl_ref[...].astype(F32), (((1,), (1,)), ((), ())),
        precision=lax.Precision.HIGHEST, preferred_element_type=F32,
    )
    pull = [jnp.broadcast_to(coupling * coef[:, f : f + 1], (M, LANES))[None] for f in range(F)]
    lane = lax.broadcasted_iota(jnp.int32, (T, M, LANES), 2)
    first, last = lane == 0, lane == LANES - 1
    below = vertical
    centre = (1.0 - 4.0 * diffusion - vertical) + below

    def advance(src, row, f, tile, after):
        rolled = pltpu.roll(tile, LANES - 1, 2)
        right = jnp.where(last, jnp.concatenate([rolled[1:], rolled[:1]], axis=0), rolled)
        rolled = pltpu.roll(tile, 1, 2)
        left = jnp.where(first, jnp.concatenate([rolled[-1:], rolled[:-1]], axis=0), rolled)
        return (
            centre * tile
            + diffusion * (src[f, row + 1] + src[f, row - 1])
            + (diffusion - advection) * right
            + (diffusion + advection) * left
            + pull[f] * after
        )

    def rows_on(src, dst, start, count, edge):
        def body(k, carry):
            row = start + k
            if edge:
                y = sl * R + row - W
                keep = jnp.where((y >= 0) & (y < slabs * R), 1.0, 0.0).astype(F32)
            tile = src[0, row]
            head = tile
            for f in range(F):
                after = src[f + 1, row] if f + 1 < F else head
                new = advance(src, row, f, tile, after)
                dst[f, row] = new * keep if edge else new
                tile = after
            return carry

        lax.fori_loop(0, count, body, 0)

    rows_on(s0, s1, W + 1, R - 2, False)
    rows_on(s1, s2, W + 2, R - 4, False)
    rows_on(s2, s3, W + 3, R - 6, False)

    def last_step(q, carry):
        row = W + 2 * q
        tiles = [s3[0, row], s3[0, row + 1]]
        heads = tiles
        for f in range(F):
            afters = [s3[f + 1, row], s3[f + 1, row + 1]] if f + 1 < F else heads
            new = [advance(s3, row + k, f, tiles[k], afters[k]) for k in range(2)]
            xs[f, :, pl.ds(pl.multiple_of(q * 2 * M, 2 * M), 2 * M), :] = jnp.concatenate(new, axis=1).astype(BF16)
            tiles = afters
        return carry


    def observe(q, carry):
        at = pl.ds(pl.multiple_of(q * 2 * M, 2 * M), 2 * M)
        cells = [jnp.broadcast_to(oc[:, pl.ds(2 * q + k, 1), :], (T, M, LANES)) for k in range(2)]
        cells = jnp.concatenate(cells, axis=1).reshape(T * 2 * M, LANES)
        kind, column = cells // LANES, lax.rem(cells, LANES)
        seen = jnp.zeros((T * 2 * M, LANES), F32)
        for f in range(F):
            tile = xs[f, :, at, :].astype(F32).reshape(T * 2 * M, LANES)
            picked = jnp.take_along_axis(tile, column, axis=1, mode="promise_in_bounds")
            seen = jnp.where(kind == f, picked, seen)
        ys[:, at, :] = seen.reshape(T, 2 * M, LANES).astype(BF16)
        return carry

    near = 1 - lax.rem(sl, 2)
    for order in range(2):
        side = near if order == 0 else 1 - near
        there = jnp.where(side == 0, sl, slabs - 1 - sl) > 0
        base = side * (W + R)

        @pl.when(there)
        def _():
            for f in range(F):
                pltpu.make_async_remote_copy(
                    src_ref=hs.at[1 - side, f], dst_ref=hr.at[side, f],
                    send_sem=halo_send.at[1 - side, f], recv_sem=halo_recv.at[side, f],
                    device_id=(mu, sl), device_id_type=MESH,
                ).wait_recv()
                for q in range(2):
                    pair = hr[side, f, q].astype(F32)
                    s0[f, base + 2 * q] = pair[:, :M]
                    s0[f, base + 2 * q + 1] = pair[:, M:]

        @pl.when(jnp.logical_not(there))
        def _():
            for f in range(F):
                for k in range(W):
                    s0[f, base + k] = jnp.zeros((T, M, LANES), F32)

        rows_on(s0, s1, 1 + 10 * side, 4, True)
        rows_on(s1, s2, 2 + 8 * side, 4, True)
        rows_on(s2, s3, 3 + 6 * side, 4, True)
        lax.fori_loop(2 * side, 2 * side + 2, last_step, 0)
        if order == 0:
            for i in range(1, M):
                oc_copy(i).wait()
        lax.fori_loop(2 * side, 2 * side + 2, observe, 0)

    def ys_copy(i):
        return pltpu.make_async_remote_copy(
            src_ref=ys.at[others[i]], dst_ref=yr.at[0, mu], send_sem=ys_send.at[i], recv_sem=ys_recv.at[i],
            device_id=(others[i], sl), device_id_type=MESH,
        )

    def xs_copy(f, i):
        fields = pl.ds(f, GROUP)
        return pltpu.make_async_remote_copy(
            src_ref=xs.at[fields, others[i]], dst_ref=xr.at[fields, mu], send_sem=xs_send.at[f, i], recv_sem=xs_recv.at[f, i],
            device_id=(others[i], sl), device_id_type=MESH,
        )

    for i in range(1, M):
        ys_copy(i).start()
    own_y = pltpu.make_async_copy(ys.at[mu], yr.at[0, mu], own_sem.at[0])
    own_y.start()
    own_x = pltpu.make_async_copy(xs.at[:, mu], xr.at[:, mu], own_sem.at[1])
    own_x.start()
    for i in range(1, M):
        xs_copy(0, i).start()

    def yf_copy(side, i):
        peer = sl - 1 if side == 0 else sl + 1
        origin = lax.rem(mu - i + M, M)
        return pltpu.make_async_remote_copy(
            src_ref=yr.at[0, origin], dst_ref=yr.at[2 - side, origin],
            send_sem=yf_send.at[side, i], recv_sem=yf_recv.at[1 - side, i],
            device_id=(mu, peer), device_id_type=MESH,
        )

    for i in range(M):
        if i == 0:
            own_y.wait()
        else:
            ys_copy(i).wait()

        @pl.when(has_low)
        def _():
            yf_copy(0, i).start()

        @pl.when(has_high)
        def _():
            yf_copy(1, i).start()

    for f in range(GROUP, F, GROUP):
        for i in range(1, M):
            xs_copy(f, i).start()

    def gram_rows(slot):
        first_row = (R, 0, 2 * R)[slot]

        def body(q, carry):
            at = pl.ds(pl.multiple_of(q * 2 * M, 2 * M), 2 * M)
            pair = yr[slot, :, at, :].astype(F32)
            for k in range(2):
                y = pair[:, k * M : (k + 1) * M, :].reshape(ENS, LANES)
                mean = jnp.sum(y, axis=0, keepdims=True) * (1.0 / ENS)
                pert = y - mean
                prec = pv[slot, 0, pl.ds(2 * q + k, 1), :]
                value = pv[slot, 1, pl.ds(2 * q + k, 1), :]
                weighted = jnp.broadcast_to(prec * (value - mean), (8, LANES))
                left = jnp.concatenate([pert * prec, weighted], axis=0)
                gs[first_row + 2 * q + k] = mm_nt(left, jnp.concatenate([pert, pert], axis=0))
            return carry

        lax.fori_loop(0, R // 2, body, 0)

    gram_rows(0)
    for side in range(2):
        there = has_low if side == 0 else has_high

        @pl.when(there)
        def _():
            pltpu.make_async_remote_copy(
                src_ref=pv.at[0], dst_ref=pv.at[1 + side], send_sem=pv_send.at[1 - side], recv_sem=pv_recv.at[side],
                device_id=(mu, sl), device_id_type=MESH,
            ).wait_recv()
            for i in range(M):
                origin = lax.rem(mu - i + M, M)
                pltpu.make_async_remote_copy(
                    src_ref=yr.at[0, origin], dst_ref=yr.at[1 + side, origin],
                    send_sem=yf_send.at[1 - side, i], recv_sem=yf_recv.at[side, i],
                    device_id=(mu, sl), device_id_type=MESH,
                ).wait_recv()

        @pl.when(jnp.logical_not(there))
        def _():
            yr[1 + side] = jnp.zeros((M, R * M, LANES), BF16)
            pv[1 + side] = jnp.zeros((2, R, LANES), F32)

        gram_rows(1 + side)

    row64 = lax.broadcasted_iota(jnp.int32, (ENS, LANES), 0)
    lane64 = lax.broadcasted_iota(jnp.int32, (ENS, LANES), 1)
    low64 = lane64 < ENS
    eye = jnp.where(lax.rem(lane64, ENS) == row64, 1.0, 0.0).astype(F32)
    y18 = lax.broadcasted_iota(jnp.int32, (24, LANES), 0)
    low18 = lax.broadcasted_iota(jnp.int32, (24, LANES), 1) < ENS
    low1 = low18[:1]

    def both(a):
        return jnp.concatenate([jnp.where(low64, a, 0.0), jnp.where(low64, 0.0, a)], axis=0)

    amats, gvecs, scales = [], [], []
    for p in range(R // 2):
        radius = jnp.where(low18, cut_ref[2 * p], cut_ref[2 * p + 1]).astype(F32)
        away = jnp.abs(y18 - jnp.where(low18, 2 * p + R, 2 * p + 1 + R)).astype(F32)
        weight = jnp.maximum(0.0, 1.0 - away / (radius + 1.0))
        total = jnp.zeros((ENS + 8, LANES), F32)
        for y in range(2 * p, 2 * p + 2 * HALO + 2):
            total = total + weight[y : y + 1] * gs[y]
        amat = (ENS - 1.0) * eye + total[:ENS]
        sums = jnp.sum(amat * amat, axis=0, keepdims=True)
        low = jnp.sum(jnp.where(low1, sums, 0.0), axis=1, keepdims=True)
        high = jnp.sum(jnp.where(low1, 0.0, sums), axis=1, keepdims=True)
        amats.append(amat)
        gvecs.append(total[ENS:])
        scales.append(jnp.sqrt(jnp.where(low1, low, high)))

    ymats = [a / s for a, s in zip(amats, scales)]
    middles = [1.5 * eye - 0.5 * y for y in ymats]
    zmats = middles
    ymats = [mm(y, both(m)) for y, m in zip(ymats, middles)]
    for step_idx in range(1, NS_STEPS):
        middles = [1.5 * eye - 0.5 * mm(z, both(y)) for z, y in zip(zmats, ymats)]
        if step_idx + 1 < NS_STEPS:
            new = [mm(jnp.concatenate([y, z], axis=0), both(m)) for y, z, m in zip(ymats, zmats, middles)]
            ymats, zmats = [n[:ENS] for n in new], [n[ENS:] for n in new]
        else:
            zmats = [mm(m, both(z)) for m, z in zip(middles, zmats)]

    source = lax.broadcasted_iota(jnp.int32, (LANES, LANES), 0)
    target = lax.broadcasted_iota(jnp.int32, (LANES, LANES), 1)
    same_row = source // ENS == lax.rem(target // M, 2)
    same_member = lax.rem(source, ENS) == (target // (2 * M)) * M + lax.rem(target, M)
    spread = jnp.where(same_row, jnp.where(same_member, 1.0 - 1.0 / ENS, -1.0 / ENS), 0.0).astype(BF16)
    odd64 = lax.rem(lane64 // M, 2) == 1
    vsum = jnp.zeros((ENS, LANES), F32)
    for p in range(R // 2):
        z, scale = both(zmats[p]), scales[p]
        wbar = mm(mm(gvecs[p], z), z)[:1] / scale
        v = math.sqrt(ENS - 1.0) * zmats[p] / jnp.sqrt(scale) + wbar
        vsum = vsum + v
        vh, vl = split(v)
        a = dot(vh, spread) + dot(vl, spread) + 1.0 / ENS
        am[p, pl.ds(2 * p, ENS, stride=R), :] = jnp.where(odd64, 0.0, a)
        am[p, pl.ds(2 * p + 1, ENS, stride=R), :] = jnp.where(odd64, a, 0.0)

    def ra_copy(i):
        return pltpu.make_async_remote_copy(
            src_ref=ps.at[others[i]], dst_ref=ra.at[mu], send_sem=ra_send.at[i], recv_sem=ra_recv.at[i],
            device_id=(others[i], sl), device_id_type=MESH,
        )


    lanes_here = pl.ds(pl.multiple_of(mu * LANES, LANES), LANES)

    def os_copy(f, i):
        return pltpu.make_async_remote_copy(
            src_ref=os_.at[f, others[i]], dst_ref=out_ref.at[:, f, :, lanes_here],
            send_sem=os_send.at[f, i], recv_sem=os_recv.at[f, i],
            device_id=(others[i], sl), device_id_type=MESH,
        )

    def own_copy(f):
        return pltpu.make_async_copy(os_.at[f, mu], out_ref.at[:, f, :, lanes_here], own_sem.at[2 + f])

    def rb_copy(i):
        peer = band * group + lax.rem(place + i, group)
        return pltpu.make_async_remote_copy(
            src_ref=rb.at[place], dst_ref=rb.at[place], send_sem=rb_send.at[i], recv_sem=rb_recv.at[i],
            device_id=(mu, peer), device_id_type=MESH,
        )

    def rc_copy(i):
        peer = lax.rem(sl + i * group, slabs)
        return pltpu.make_async_remote_copy(
            src_ref=rc.at[band], dst_ref=rc.at[band], send_sem=rc_send.at[i], recv_sem=rc_recv.at[i],
            device_id=(mu, peer), device_id_type=MESH,
        )

    own_x.wait()
    for f in range(F):
        if f % GROUP == 0:
            for i in range(1, M):
                xs_copy(f, i).wait()
        tiles = [xr[f, :, q * 2 * M : (q + 1) * 2 * M, :].reshape(2 * ENS, LANES) for q in range(R // 2)]
        field = jnp.concatenate(tiles, axis=0)
        for h in range(4):
            ah, al = split(jnp.concatenate([am[p, h * LANES : (h + 1) * LANES, :] for p in range(R // 2)], axis=1))
            new = dot(ah, field) + dot(al, field)
            os_[f, 2 * h : 2 * h + 2] = new.reshape(2, M, R, LANES).astype(BF16)
        for i in range(1, M):
            os_copy(f, i).start()
        own_copy(f).start()
        if f == 0:
            for i in range(1, M):
                pp_copy(i).wait()
            every = pp[...].reshape(ENS, LANES)
            pbar = jnp.sum(every, axis=0, keepdims=True) * (1.0 / ENS)
            ppert = every - pbar
            ps[...] = mm(vsum, jnp.concatenate([ppert, ppert], axis=0)).reshape(M, M, LANES)
            for i in range(1, M):
                ra_copy(i).start()
            ra[mu] = ps[mu]

        if f == STAGE_AT[0]:
            for i in range(1, M):
                ra_copy(i).wait()
            rb[place] = jnp.sum(ra[...], axis=0)
            for i in range(1, group):
                rb_copy(i).start()
        if f == STAGE_AT[1]:
            for i in range(1, group):
                rb_copy(i).wait()
            rc[band] = jnp.sum(rb[...], axis=0)
            for i in range(1, bands):
                rc_copy(i).start()

    for i in range(1, bands):
        rc_copy(i).wait()
    total = jnp.sum(rc[...], axis=0) * (1.0 / (slabs * R * M)) + pbar
    pout_ref[...] = total[:, : pout_ref.shape[1]]

    for f in range(F):
        for i in range(1, M):
            os_copy(f, i).wait()
        own_copy(f).wait()
    for side in range(2):
        there = has_low if side == 0 else has_high

        @pl.when(there)
        def _():
            for f in range(F):
                halo_copy(side, f).wait_send()
            pv_copy(side).wait_send()
            for i in range(M):
                yf_copy(side, i).wait_send()


def local(prior_ensemble_fields, params, influence, obs_cell, obs_value, obs_prec, cutoff):
    slabs = lax.axis_size("slab")
    group = 8 if slabs % 8 == 0 else slabs
    bands = slabs // group
    npar = params.shape[1]
    vmem = pl.BlockSpec(memory_space=pltpu.VMEM)
    dma = pltpu.SemaphoreType.DMA
    ext = R + 2 * W
    analysis, param_analysis = pl.pallas_call(
        lambda *refs: kernel(slabs, group, *refs),
        out_shape=(
            pltpu.VMEM((M, F, R, T * LANES), BF16),
            pltpu.VMEM((M, npar), F32),
        ),
        in_specs=[
            pl.BlockSpec(memory_space=pl.ANY), vmem, vmem, vmem, vmem, vmem,
            pl.BlockSpec(memory_space=pltpu.SMEM),
        ],
        out_specs=(vmem, vmem),
        scratch_shapes=[
            pltpu.VMEM((F, ext, T, M, LANES), F32),
            pltpu.VMEM((F, ext, T, M, LANES), F32),
            pltpu.VMEM((F, ext, T, M, LANES), F32),
            pltpu.VMEM((F, ext, T, M, LANES), F32),
            pltpu.VMEM((2, F, 2, T, 2 * M, LANES), BF16),
            pltpu.VMEM((2, F, 2, T, 2 * M, LANES), BF16),
            pltpu.VMEM((F, T, R * M, LANES), BF16),
            pltpu.VMEM((F, M, R * M, LANES), BF16),
            pltpu.VMEM((T, R * M, LANES), BF16),
            pltpu.VMEM((3, M, R * M, LANES), BF16),
            pltpu.VMEM((M, R, LANES), jnp.int32),
            pltpu.VMEM((3, 2, R, LANES), F32),
            pltpu.VMEM((M, M, LANES), F32),
            pltpu.VMEM((3 * R, ENS + 8, LANES), F32),
            pltpu.VMEM((R // 2, ENS * R, LANES), F32),
            pltpu.VMEM((F, M, M, R, LANES), BF16),
            pltpu.VMEM((M, M, LANES), F32),
            pltpu.VMEM((M, M, LANES), F32),
            pltpu.VMEM((group, M, LANES), F32),
            pltpu.VMEM((bands, M, LANES), F32),
            dma((F, M)), dma((2, F)), dma((2, F)), dma((2,)), dma((2,)),
            dma((M,)), dma((M,)), dma((M,)), dma((M,)),
            dma((M,)), dma((M,)), dma((2, M)), dma((2, M)), dma((F, M)), dma((F, M)), dma((F, M)), dma((F, M)),
            dma((M,)), dma((M,)), dma((group,)), dma((group,)), dma((bands,)), dma((bands,)), dma((2 + F,)),
        ],
        compiler_params=pltpu.CompilerParams(
            collective_id=0, has_side_effects=True, vmem_limit_bytes=56 * 1024 * 1024
        ),
        name="cycle",
    )(
        prior_ensemble_fields.reshape(M, F, R, T, LANES),
        params,
        influence.T,
        obs_cell.reshape(R, LANES),
        obs_value.reshape(R, LANES),
        obs_prec.reshape(R, LANES),
        cutoff,
    )
    return analysis.reshape(M, F, R, 1, T * LANES), param_analysis


def solution(mesh):
    in_specs = (
        P("member", None, "slab", None, None),
        P("member", None),
        P(),
        P("slab", "member", None),
        P("slab", "member", None),
        P("slab", "member", None),
        P("slab"),
    )
    out_specs = (P("member", None, "slab", None, None), P("member", None))
    return jax.shard_map(local, mesh=mesh, in_specs=in_specs, out_specs=out_specs, check_vma=False)
```
